256 devices in a mesh: src: 4 (over z_hi), gx: 16 (over z_lo, y, core), gy: 4 (over x).
Axes of the slice: x: 4, y: 4, z: 8 (z_hi: 4, z_lo: 2; z = z_hi * 2 + z_lo), core: 2. Of those that a mesh axis runs over, the one named last changes fastest.
Arguments:
- adjoint_now: float32 [4, 2, 64, 128, 512], P('src', None, 'gx', 'gy'), may hold values from -6 to 6
- adjoint_before: float32 [4, 2, 64, 128, 512], P('src', None, 'gx', 'gy'), may hold values from -6 to 6
- forward_field: bfloat16 [3, 4, 2, 64, 128, 512], P(None, 'src', None, 'gx', 'gy'), may hold values from -6 to 6
- velocity: float32 [64, 128, 512], P('gx', 'gy'), may hold values from 0.2 to 0.4
- thomsen_eps: float32 [64, 128, 512], P('gx', 'gy'), may hold values from 0.05 to 0.35
- thomsen_delta: float32 [64, 128, 512], P('gx', 'gy'), may hold values from 0 to 0.25
- tilt_level: int32 [64, 128, 512], P('gx', 'gy'), may hold values from 0 to 31
- azimuth_level: int32 [64, 128, 512], P('gx', 'gy'), may hold values from 0 to 31
- channel_cell: int32 [4, 1536], P('src'), may hold values from 0 to 8191
- channel_count: int32 [4], P('src'), may hold values from 512 to 1536, as said below
- residual_trace: float32 [4, 3, 1536], P('src'), may hold values from -6 to 6
Outputs:
- adjoint_next: float32 [4, 2, 64, 128, 512], P('src', None, 'gx', 'gy')
- grad_velocity: float32 [64, 128, 512], P('gx', 'gy', 'src')
- grad_epsilon: float32 [64, 128, 512], P('gx', 'gy', 'src')
- grad_delta: float32 [64, 128, 512], P('gx', 'gy', 'src')
The draws below stay inside these ranges and needn't reach their ends.
Inputs may be any that keep to these rules, and one draw needn't show every extreme that they name: `channel_count`: some virtual source has 1536 live channels and some other has 512.
All inputs are finite; a program needn't handle non-finite values.
Results may differ from the reference program's by a relative error of at most 0.0003.
Values sent between devices are 32-bit elements; how exact they have to be, the bound alone decides.
A program may use at most 64 MiB of HBM per device.

```python
import math
import jax
import jax.numpy as jnp

NZ = 512
STEPS = 3
LEVELS = 32
CH_MAX = 1536
NX = 64
NY = 128
SOURCES = 4


def draw_channel_count(key, part):
    key_base = jax.random.fold_in(key, 11)
    key_most = jax.random.fold_in(key, 12)
    key_least = jax.random.fold_in(key, 13)
    counts_base = jax.random.randint(key_base, (SOURCES,), CH_MAX // 3, CH_MAX + 1)
    busiest = jax.random.randint(key_most, (), 0, SOURCES)
    offset_draw = jax.random.randint(key_least, (), 0, SOURCES - 1)
    lightest = (busiest + 1 + offset_draw) % SOURCES
    counts_base = counts_base.at[busiest].set(CH_MAX)
    counts_base = counts_base.at[lightest].set(CH_MAX // 3)
    return counts_base.astype(jnp.int32)


def plant(entries, stream_key, least, top_value):
    place = [jax.random.randint(jax.random.fold_in(stream_key, axis), (), 0, length) for axis, length in enumerate(entries.shape)]
    longest = entries.shape.index(max(entries.shape))
    beside = place[:longest] + [(place[longest] + 1) % entries.shape[longest]] + place[longest + 1:]
    return entries.at[tuple(place)].set(least).at[tuple(beside)].set(top_value)


def steps_of(own_key, shape, cuts, smallest, high):
    factor_of, own = 1.0, jax.random.fold_in(own_key, 6)
    for dim, shards_of in cuts:
        steps = jnp.exp(jax.random.uniform(jax.random.fold_in(own, dim), (shards_of,), jnp.float32, smallest / len(cuts), high / len(cuts)))
        factor_of = factor_of * jnp.repeat(steps, shape[dim] // shards_of).reshape([-1 if axis == dim else 1 for axis in range(len(shape))])
    return factor_of


def bell_draw(own_key, shape, deviation, limit, pieces=(), kind=jnp.bfloat16):
    level = steps_of(own_key, shape, pieces, -0.22, 0.18) if pieces else 1.0
    drawn = jax.random.normal(own_key, shape, jnp.float32) * deviation * level
    return jnp.minimum(jnp.maximum(drawn, -limit), limit).astype(kind)


def setup_inputs(seed: int = 0) -> dict:
    splits = jax.random.split(jax.random.key(seed), 12)
    adjoint_now = bell_draw(splits[0], (SOURCES, 2, NX, NY, NZ), 1.0, 6.0, ((0, 4), (2, 16), (3, 4)), jnp.float32)
    adjoint_before = bell_draw(splits[1], (SOURCES, 2, NX, NY, NZ), 1.0, 6.0, ((0, 4), (2, 16), (3, 4)), jnp.float32)
    forward_field = bell_draw(splits[2], (STEPS, SOURCES, 2, NX, NY, NZ), 1.0, 6.0, ((1, 4), (3, 16), (4, 4)))
    velocity = jnp.clip(jnp.exp(math.log(0.4) - 0.6931472 * jax.random.uniform(splits[3], (NX, NY, NZ), jnp.float32) ** steps_of(splits[3], (NX, NY, NZ), ((0, 16), (1, 4)), -0.2, 0.2)), 0.2, 0.4)
    thomsen_eps = jnp.clip(0.05 + 0.29999999 * jax.random.uniform(splits[4], (NX, NY, NZ), jnp.float32) ** steps_of(splits[4], (NX, NY, NZ), ((0, 16), (1, 4)), -0.2, 0.2), 0.05, 0.35)
    thomsen_delta = jnp.clip(0.25 * jax.random.uniform(splits[5], (NX, NY, NZ), jnp.float32) ** steps_of(splits[5], (NX, NY, NZ), ((0, 16), (1, 4)), -0.2, 0.2), 0.0, 0.25)
    tilt_level = plant(jax.random.randint(splits[6], (NX, NY, NZ), 0, LEVELS), jax.random.fold_in(splits[6], 1), 0, LEVELS - 1).astype(jnp.int32)
    azimuth_level = plant(jax.random.randint(splits[7], (NX, NY, NZ), 0, LEVELS), jax.random.fold_in(splits[7], 1), 0, LEVELS - 1).astype(jnp.int32)
    channel_cell = plant(jax.random.randint(splits[8], (SOURCES, CH_MAX), 0, NX * NY), jax.random.fold_in(splits[8], 1), 0, (NX * NY) - 1).astype(jnp.int32)
    channel_count = draw_channel_count(jax.random.fold_in(splits[11], 71), 0)
    residual_trace = bell_draw(splits[10], (SOURCES, STEPS, CH_MAX), 1.0, 6.0, ((0, 4),), jnp.float32)
    return dict(adjoint_now=adjoint_now, adjoint_before=adjoint_before, forward_field=forward_field, velocity=velocity, thomsen_eps=thomsen_eps, thomsen_delta=thomsen_delta, tilt_level=tilt_level, azimuth_level=azimuth_level, channel_cell=channel_cell, channel_count=channel_count, residual_trace=residual_trace)


def derivatives(padded):
    center = padded[..., 1:-1, 1:-1, 1:-1]
    second_x = padded[..., 2:, 1:-1, 1:-1] + padded[..., :-2, 1:-1, 1:-1] - 2.0 * center
    second_y = padded[..., 1:-1, 2:, 1:-1] + padded[..., 1:-1, :-2, 1:-1] - 2.0 * center
    second_z = padded[..., 1:-1, 1:-1, 2:] + padded[..., 1:-1, 1:-1, :-2] - 2.0 * center
    mixed_xy = 0.25 * (padded[..., 2:, 2:, 1:-1] - padded[..., 2:, :-2, 1:-1] - padded[..., :-2, 2:, 1:-1] + padded[..., :-2, :-2, 1:-1])
    mixed_yz = 0.25 * (padded[..., 1:-1, 2:, 2:] - padded[..., 1:-1, 2:, :-2] - padded[..., 1:-1, :-2, 2:] + padded[..., 1:-1, :-2, :-2])
    mixed_xz = 0.25 * (padded[..., 2:, 1:-1, 2:] - padded[..., 2:, 1:-1, :-2] - padded[..., :-2, 1:-1, 2:] + padded[..., :-2, 1:-1, :-2])
    return (second_x, second_y, second_z, mixed_xy, mixed_yz, mixed_xz)

def tilt_weights(tilt_level, azimuth_level):
    theta = tilt_level.astype(jnp.float32) * (0.5 * math.pi / LEVELS)
    azimuth = azimuth_level.astype(jnp.float32) * (2.0 * math.pi / LEVELS)
    sin_t = jnp.sin(theta)
    cos_t = jnp.cos(theta)
    sin_p = jnp.sin(azimuth)
    cos_p = jnp.cos(azimuth)
    return (sin_t * sin_t * cos_p * cos_p, sin_t * sin_t * sin_p * sin_p, cos_t * cos_t, 2.0 * sin_t * sin_t * sin_p * cos_p, 2.0 * sin_t * cos_t * sin_p, 2.0 * sin_t * cos_t * cos_p)

def split_operators(padded, weights):
    parts = derivatives(padded)
    axial = weights[0] * parts[0]
    for index in range(1, 6):
        axial = axial + weights[index] * parts[index]
    laplace = parts[0] + parts[1] + parts[2]
    return (laplace[..., 0, :, :, :] - axial[..., 0, :, :, :], axial[..., 1, :, :, :])

def reference(adjoint_now, adjoint_before, forward_field, velocity, thomsen_eps, thomsen_delta, tilt_level, azimuth_level, channel_cell, channel_count, residual_trace):
    weights = tilt_weights(tilt_level, azimuth_level)
    speed_sq = velocity * velocity
    stretch = 1.0 + 2.0 * thomsen_eps
    root = jnp.sqrt(1.0 + 2.0 * thomsen_delta)
    live = jnp.arange(CH_MAX, dtype=jnp.int32)[None, :] < channel_count[:, None]
    loads = jnp.where(live[:, None, :], residual_trace, jnp.zeros_like(residual_trace))
    rows_src = jnp.arange(SOURCES, dtype=jnp.int32)[:, None, None]
    rows_time = jnp.arange(STEPS, dtype=jnp.int32)[None, :, None]
    surface = jnp.zeros((SOURCES, STEPS, NX * NY), residual_trace.dtype)
    surface = surface.at[rows_src, rows_time, channel_cell[:, None, :]].add(loads)
    surface = surface.reshape(SOURCES, STEPS, NX, NY)
    grad_velocity = jnp.zeros_like(velocity)
    grad_epsilon = jnp.zeros_like(velocity)
    grad_delta = jnp.zeros_like(velocity)
    finals = []
    for source in range(SOURCES):
        current = adjoint_now[source]
        previous = adjoint_before[source]
        for time_step in range(STEPS):
            padded = jnp.pad(current, ((0, 0), (1, 1), (1, 1), (1, 1)))
            horiz_p, axial_q = split_operators(padded, weights)
            update_p = stretch * horiz_p + root * axial_q
            update_q = root * horiz_p + axial_q
            following = 2.0 * current - previous + speed_sq * jnp.stack([update_p, update_q])
            following = following.at[0, :, :, 0].add(surface[source, time_step])
            forward_p = forward_field[time_step, source, 0].astype(jnp.float32)
            forward_q = forward_field[time_step, source, 1].astype(jnp.float32)
            grad_velocity = grad_velocity + 2.0 * velocity * (forward_p * update_p + forward_q * update_q)
            grad_epsilon = grad_epsilon + 2.0 * speed_sq * forward_p * horiz_p
            grad_delta = grad_delta + speed_sq / root * (forward_p * axial_q + forward_q * horiz_p)
            previous = current
            current = following
        finals.append(current)
    return (jnp.stack(finals), grad_velocity, grad_epsilon, grad_delta)
```

```python
import functools
import math

import jax
import jax.numpy as jnp
from jax import lax
from jax.experimental import pallas as pl
from jax.experimental.pallas import tpu as pltpu
from jax.sharding import PartitionSpec as P

LEVELS = 32
LANES = 128
ROWS = 8
TOP = 8
MESH = pl.DeviceIdType.MESH
F32 = jnp.float32
BF16 = jnp.bfloat16


def sin_cos_small(angle):
    sq = angle * angle
    sin = angle + angle * sq * (-1.0 / 6 + sq * (1.0 / 120 + sq * (-1.0 / 5040 + sq * (1.0 / 362880))))
    cos = 1.0 + sq * (-0.5 + sq * (1.0 / 24 + sq * (-1.0 / 720 + sq * (1.0 / 40320 - sq * (1.0 / 3628800)))))
    return sin, cos


def kernel(
    size_x,
    size_y,
    size_s,
    width_y,
    now_hbm,
    before_hbm,
    forward_hbm,
    vel_hbm,
    eps_hbm,
    delta_hbm,
    tilt_hbm,
    azimuth_hbm,
    cell_hbm,
    count_ref,
    trace_hbm,
    next_hbm,
    gvel_hbm,
    geps_hbm,
    gdelta_hbm,
    field,
    before,
    forward,
    params,
    levels,
    own,
    cells,
    traces,
    parts,
    coef,
    surf,
    ha,
    sums,
    edge_out,
    edge_in,
    corner_in,
    far_in,
    near_in,
    result,
    grads,
    load_sem,
    out_sem,
    xs,
    xr,
    ys,
    yr,
    cs,
    cr,
    fs,
    fr,
    ns,
    nr,
):
    gx, gy, me = lax.axis_index("gx"), lax.axis_index("gy"), lax.axis_index("src")
    steps = 3
    nx = now_hbm.shape[2]
    ny = now_hbm.shape[3]
    nzb = now_hbm.shape[4] // LANES
    tiles = ny // ROWS
    body = pl.ds(TOP, ny)
    has_x = (gx > 0, gx < size_x - 1)
    has_y = (gy > 0, gy < size_y - 1)
    to_x = (gx - 1, gx + 1)
    to_y = (gy - 1, gy + 1)
    up = lax.rem(me + 1, size_s)
    down = lax.rem(me + size_s - 1, size_s)
    across = lax.rem(me + 2, size_s)

    def lanes_of(zb):
        return pl.ds(zb * LANES, LANES)

    loads = {}

    def load(name, index, src, dst):
        loads.setdefault(name, []).append(pltpu.make_async_copy(src, dst, load_sem.at[index]))

    for zb in range(nzb):
        load("now", zb, now_hbm.at[0, :, :, :, lanes_of(zb)], field.at[0, zb, :, pl.ds(1, nx), body, :])
    load("angle", nzb, tilt_hbm, levels.at[0])
    load("angle", nzb + 1, azimuth_hbm, levels.at[1])
    load("params", nzb + 2, vel_hbm, params.at[0])
    load("params", nzb + 3, eps_hbm, params.at[1])
    load("params", nzb + 4, delta_hbm, params.at[2])
    load("channels", nzb + 5, cell_hbm, cells)
    load("channels", nzb + 6, trace_hbm.at[0], traces)
    load("before", nzb + 7, before_hbm.at[0], before)
    load("forward", nzb + 8, forward_hbm.at[:, 0], forward)
    mine = pl.ds(pl.multiple_of(me * LANES, LANES), LANES)
    load("own", nzb + 9, vel_hbm.at[:, :, mine], own.at[0])
    load("own", nzb + 10, eps_hbm.at[:, :, mine], own.at[1])
    load("own", nzb + 11, delta_hbm.at[:, :, mine], own.at[2])
    for group in loads.values():
        for copy in group:
            copy.start()

    def arrived(name):
        for copy in loads[name]:
            copy.wait()

    barrier = pltpu.get_barrier_semaphore()
    greeted = jnp.int32(2)
    for dx in (0, 1):
        @pl.when(has_x[dx])
        def _():
            pl.semaphore_signal(barrier, inc=1, device_id={"gx": to_x[dx]}, device_id_type=MESH)
        greeted = greeted + has_x[dx].astype(jnp.int32)
    for dy in (0, 1):
        @pl.when(has_y[dy])
        def _():
            pl.semaphore_signal(barrier, inc=1, device_id={"gy": to_y[dy]}, device_id_type=MESH)
        greeted = greeted + has_y[dy].astype(jnp.int32)
    for dx in (0, 1):
        for dy in (0, 1):
            both = has_x[dx] & has_y[dy]
            @pl.when(both)
            def _():
                pl.semaphore_signal(
                    barrier, inc=1, device_id={"gx": to_x[dx], "gy": to_y[dy]}, device_id_type=MESH
                )
            greeted = greeted + both.astype(jnp.int32)
    for peer in (up, down):
        pl.semaphore_signal(barrier, inc=1, device_id={"src": peer}, device_id_type=MESH)

    for dx in (0, 1):
        @pl.when(jnp.logical_not(has_x[dx]))
        def _():
            plane = (0, nx + 1)[dx]
            zeros = jnp.zeros((ny + 2 * TOP, LANES), F32)
            @pl.loop(0, steps)
            def _(t):
                for zb in range(nzb):
                    for c in (0, 1):
                        field[t, zb, c, plane] = zeros
    for dy in (0, 1):
        @pl.when(jnp.logical_not(has_y[dy]))
        def _():
            row = (TOP - 1, TOP + ny)[dy]
            zeros = jnp.zeros((1, LANES), F32)
            @pl.loop(0, steps)
            def _(t):
                for zb in range(nzb):
                    for c in (0, 1):
                        for x in range(nx + 2):
                            field[t, zb, c, x, pl.ds(row, 1)] = zeros
    pl.semaphore_wait(barrier, greeted)

    def face(t, dx):
        return pltpu.make_async_remote_copy(
            src_ref=field.at[t, :, :, (1, nx)[dx], body, :],
            dst_ref=field.at[t, :, :, (nx + 1, 0)[dx], body, :],
            send_sem=xs.at[t, dx],
            recv_sem=xr.at[t, dx],
            device_id={"gx": to_x[dx]},
            device_id_type=MESH,
        )

    def first_face(zb, dx):
        return pltpu.make_async_remote_copy(
            src_ref=now_hbm.at[0, :, (0, nx - 1)[dx], :, lanes_of(zb)],
            dst_ref=field.at[0, zb, :, (nx + 1, 0)[dx], body, :],
            send_sem=xs.at[0, dx],
            recv_sem=xr.at[0, dx],
            device_id={"gx": to_x[dx]},
            device_id_type=MESH,
        )

    def edge(t, dy):
        return pltpu.make_async_remote_copy(
            src_ref=edge_out.at[t, dy],
            dst_ref=edge_in.at[t, dy],
            send_sem=ys.at[t, dy],
            recv_sem=yr.at[t, dy],
            device_id={"gy": to_y[dy]},
            device_id_type=MESH,
        )

    def corner(t, dx, dy):
        return pltpu.make_async_remote_copy(
            src_ref=edge_out.at[t, dy, (0, nx - 1)[dx]],
            dst_ref=corner_in.at[t, dx, dy],
            send_sem=cs.at[t, dx, dy],
            recv_sem=cr.at[t, dx, dy],
            device_id={"gx": to_x[dx], "gy": to_y[dy]},
            device_id_type=MESH,
        )

    def send_faces(t):
        for dx in (0, 1):
            @pl.when(has_x[dx])
            def _():
                face(t, dx).start()

    def send_edges(t):
        for x in range(nx):
            for zb in range(nzb):
                for c in (0, 1):
                    slot = pl.ds(zb * 2 + c, 1)
                    edge_out[t, 0, x, slot] = field[t, zb, c, x + 1, pl.ds(TOP, 1)]
                    edge_out[t, 1, x, slot] = field[t, zb, c, x + 1, pl.ds(TOP + ny - 1, 1)]
        for dy in (0, 1):
            @pl.when(has_y[dy])
            def _():
                edge(t, dy).start()
        for dx in (0, 1):
            for dy in (0, 1):
                @pl.when(has_x[dx] & has_y[dy])
                def _():
                    corner(t, dx, dy).start()

    def receive_edges(t):
        for dy in (0, 1):
            @pl.when(has_y[1 - dy])
            def _():
                edge(t, dy).wait_recv()
                row = (TOP + ny, TOP - 1)[dy]
                for x in range(nx):
                    for zb in range(nzb):
                        for c in (0, 1):
                            field[t, zb, c, x + 1, pl.ds(row, 1)] = edge_in[t, dy, x, pl.ds(zb * 2 + c, 1)]

    def receive_faces(t):
        for dx in (0, 1):
            for dy in (0, 1):
                @pl.when(has_x[1 - dx] & has_y[1 - dy])
                def _():
                    corner(t, dx, dy).wait_recv()
                    row = (TOP + ny, TOP - 1)[dy]
                    for zb in range(nzb):
                        for c in (0, 1):
                            field[t, zb, c, (nx + 1, 0)[dx], pl.ds(row, 1)] = corner_in[
                                t, dx, dy, pl.ds(zb * 2 + c, 1)
                            ]
        for dx in (0, 1):
            @pl.when(has_x[1 - dx])
            def _():
                face(t, dx).wait_recv()

    for dx in (0, 1):
        @pl.when(has_x[dx])
        def _():
            for zb in range(nzb):
                first_face(zb, dx).start()
    arrived("now")
    send_edges(0)

    arrived("angle")
    arrived("params")

    @pl.loop(0, nx)
    def _(x):
        for tile in range(tiles):
            rows = pl.ds(tile * ROWS, ROWS)
            for zb in range(nzb):
                cols = lanes_of(zb)
                tilt = levels[0, x, rows, cols].astype(F32)
                turn = levels[1, x, rows, cols].astype(F32)
                sin_h, cos_h = sin_cos_small(tilt * (0.5 * math.pi / LEVELS) - 0.25 * math.pi)
                sin_t = (sin_h + cos_h) * math.sqrt(0.5)
                cos_t = (cos_h - sin_h) * math.sqrt(0.5)
                sin_q, cos_q = sin_cos_small(turn * (0.5 * math.pi / LEVELS) - 0.25 * math.pi)
                sin_2, cos_2 = 2.0 * sin_q * cos_q, 1.0 - 2.0 * sin_q * sin_q
                sin_p, cos_p = -2.0 * sin_2 * cos_2, 2.0 * sin_2 * sin_2 - 1.0
                flat = sin_t * sin_t
                slope = 0.5 * sin_t * cos_t
                coef[0, x, zb, rows] = flat * cos_p * cos_p
                coef[1, x, zb, rows] = flat * sin_p * sin_p
                coef[2, x, zb, rows] = cos_t * cos_t
                coef[3, x, zb, rows] = 0.5 * flat * sin_p * cos_p
                coef[4, x, zb, rows] = slope * sin_p
                coef[5, x, zb, rows] = slope * cos_p
                vel = params[0, x, rows, cols]
                coef[6, x, zb, rows] = vel * vel
                coef[7, x, zb, rows] = 1.0 + 2.0 * params[1, x, rows, cols]
                coef[8, x, zb, rows] = jnp.sqrt(1.0 + 2.0 * params[2, x, rows, cols])

    arrived("channels")
    cell = cells[...]
    local_x = cell // width_y - gx * nx
    local_y = cell % width_y - gy * ny
    slots = lax.broadcasted_iota(jnp.int32, cell.shape, 1)
    inside = (local_x >= 0) & (local_x < nx) & (local_y >= 0) & (local_y < ny) & (slots < count_ref[0])
    target = jnp.where(inside, local_x * ny + local_y, -1)
    spots = lax.broadcasted_iota(jnp.int32, (nx * ny, cell.shape[1]), 0)
    onehot = jnp.where(target == spots, 1.0, 0.0).astype(BF16)
    value = traces[...]
    high = value.astype(BF16).astype(F32)
    middle = (value - high).astype(BF16).astype(F32)
    low = (value - high) - middle
    parts[...] = jnp.zeros_like(parts)
    parts[pl.ds(0, steps)] = high
    parts[pl.ds(steps, steps)] = middle
    parts[pl.ds(2 * steps, steps)] = low
    table = lax.dot_general(
        onehot, parts[...].astype(BF16), (((1,), (1,)), ((), ())), preferred_element_type=F32
    )
    table = table + pltpu.roll(table, LANES - steps, 1) + pltpu.roll(table, LANES - 2 * steps, 1)
    spot_lane = lax.broadcasted_iota(jnp.int32, table.shape, 1)
    for t in range(steps):
        moved = table if t == 0 else pltpu.roll(table, LANES - t, 1)
        surf[t] = jnp.where(spot_lane == 0, moved, 0.0)

    lane = lax.broadcasted_iota(jnp.int32, (ROWS, LANES), 1)
    first, last = lane == 0, lane == LANES - 1
    zero = jnp.zeros((ROWS, LANES), F32)

    def shifted(blocks):
        ahead = [pltpu.roll(block, LANES - 1, 1) for block in blocks] + [zero]
        behind = [zero] + [pltpu.roll(block, 1, 1) for block in blocks]
        after = [jnp.where(last, ahead[i + 1], ahead[i]) for i in range(nzb)]
        prior = [jnp.where(first, behind[i], behind[i + 1]) for i in range(nzb)]
        return after, prior

    def stencil(t, c, x, tile, weights):
        def read(dx, dy):
            rows = pl.ds(TOP + tile * ROWS + dy, ROWS)
            return [field[t, zb, c, x + 1 + dx, rows] for zb in range(nzb)]

        center, right, left, north, south = read(0, 0), read(1, 0), read(-1, 0), read(0, 1), read(0, -1)
        slope_y = [a - b for a, b in zip(north, south)]
        slope_x = [a - b for a, b in zip(right, left)]
        cross = [(a - b) - (d - e) for a, b, d, e in zip(read(1, 1), read(1, -1), read(-1, 1), read(-1, -1))]
        after, prior = shifted(center)
        after_y, prior_y = shifted(slope_y)
        after_x, prior_x = shifted(slope_x)
        out = []
        for zb in range(nzb):
            w = weights[zb]
            sum_x = right[zb] + left[zb]
            sum_y = north[zb] + south[zb]
            sum_z = after[zb] + prior[zb]
            mixed = (
                w[0] * sum_x
                + w[1] * sum_y
                + w[2] * sum_z
                + w[3] * cross[zb]
                + w[4] * (after_y[zb] - prior_y[zb])
                + w[5] * (after_x[zb] - prior_x[zb])
            )
            twice = center[zb] + center[zb]
            if c == 0:
                out.append((sum_x + sum_y + sum_z) - (twice + twice) - mixed)
            else:
                out.append(mixed - twice)
        return out

    def advance(t, x, tile):
        rows = pl.ds(tile * ROWS, ROWS)
        for zb in range(nzb):
            cols = lanes_of(zb)
            horiz, axial = ha[0, x, zb, rows], ha[1, x, zb, rows]
            speed, stretch, root = (coef[i, x, zb, rows] for i in (6, 7, 8))
            updates = (stretch * horiz + root * axial, root * horiz + axial)
            for c in (0, 1):
                here = pl.ds(TOP + tile * ROWS, ROWS)
                center = field[t, zb, c, x + 1, here]
                old = before[c, x, rows, cols] if t == 0 else field[t - 1, zb, c, x + 1, here]
                following = (center + center) - old + speed * updates[c]
                if zb == 0 and c == 0:
                    start = pl.multiple_of(x * ny + tile * ROWS, ROWS)
                    following = following + surf[t, pl.ds(start, ROWS)]
                if t == steps - 1:
                    result[c, x, rows, cols] = following
                else:
                    field[t + 1, zb, c, x + 1, here] = following

    def operators(t, x):
        for tile in range(tiles):
            rows = pl.ds(tile * ROWS, ROWS)
            weights = [[coef[i, x, zb, rows] for i in range(6)] for zb in range(nzb)]
            for c in (0, 1):
                out = stencil(t, c, x, tile, weights)
                for zb in range(nzb):
                    ha[c, x, zb, rows] = out[zb]
            if t < steps - 1:
                advance(t, x, tile)

    def accumulate(t, x):
        for half in range(ny // 16):
            rows = pl.ds(half * 16, 16)
            for zb in range(nzb):
                cols = lanes_of(zb)
                horiz, axial = ha[0, x, zb, rows], ha[1, x, zb, rows]
                pf = forward[t, 0, x, rows, cols].astype(F32)
                qf = forward[t, 1, x, rows, cols].astype(F32)
                terms = (pf * horiz, pf * axial + qf * horiz, qf * axial)
                for i in range(3):
                    sums[zb, i, x, rows] = terms[i] if t == 0 else sums[zb, i, x, rows] + terms[i]

    half = nx // 2
    inner, outer = list(range(1, nx - 1)), [0, nx - 1]

    def far(x):
        way = 0 if x < half else 1
        return pltpu.make_async_remote_copy(
            src_ref=sums.at[across, :, x],
            dst_ref=far_in.at[x],
            send_sem=fs.at[x],
            recv_sem=fr.at[x],
            device_id={"src": (up, down)[way]},
            device_id_type=MESH,
        )

    def near(x, way):
        return pltpu.make_async_remote_copy(
            src_ref=sums.at[(up, down)[way], :, x],
            dst_ref=near_in.at[way, x],
            send_sem=ns.at[way, x],
            recv_sem=nr.at[way, x],
            device_id={"src": (up, down)[way]},
            device_id_type=MESH,
        )

    arrived("before")
    for t in range(steps):
        final = t == steps - 1

        def plane(x):
            operators(t, x)
            if final:
                accumulate(t, x)

        receive_edges(t)

        @pl.loop(1, nx - 1)
        def _(x):
            plane(x)

        if final:
            for x in inner:
                far(x).start()
            for x in inner:
                near(x, 1 if x < half else 0).start()
        receive_faces(t)
        if not final:
            @pl.loop(0, 2)
            def _(i):
                plane(i * (nx - 1))

            send_faces(t + 1)
            send_edges(t + 1)
            if t == 0:
                arrived("forward")

            @pl.loop(0, nx)
            def _(x):
                accumulate(t, x)
        else:
            @pl.loop(0, 2)
            def _(i):
                plane(i * (nx - 1))

    for x in outer:
        far(x).start()
    for x in outer:
        near(x, 1 if x < half else 0).start()

    @pl.loop(0, nx)
    def _(x):
        for tile in range(tiles):
            advance(steps - 1, x, tile)

    out_copy = pltpu.make_async_copy(result, next_hbm.at[0], out_sem.at[0])
    out_copy.start()
    for x in inner + outer:
        way = 0 if x < half else 1
        far(x).wait_recv()
        for i in range(3):
            sums[(up, down)[way], i, x] = sums[(up, down)[way], i, x] + far_in[x, i]
        near(x, way).start()

    arrived("own")
    for x in inner + outer:
        for way in (0, 1):
            near(x, way).wait_recv()
        for tile in range(tiles):
            rows = pl.ds(tile * ROWS, ROWS)
            a, b, c = (
                sums[me, i, x, rows] + near_in[0, x, i, rows] + near_in[1, x, i, rows] for i in range(3)
            )
            vel = own[0, x, rows]
            stretch = 1.0 + 2.0 * own[1, x, rows]
            root = jnp.sqrt(1.0 + 2.0 * own[2, x, rows])
            speed = vel * vel
            grads[0, x, rows] = 2.0 * vel * (stretch * a + root * b + c)
            grads[1, x, rows] = 2.0 * speed * a
            grads[2, x, rows] = speed / root * b
    grad_copies = [
        pltpu.make_async_copy(grads.at[i], out, out_sem.at[1 + i])
        for i, out in enumerate((gvel_hbm, geps_hbm, gdelta_hbm))
    ]
    for copy in grad_copies:
        copy.start()

    for t in range(steps):
        for dx in (0, 1):
            @pl.when(has_x[dx])
            def _():
                face(t, dx).wait_send()
        for dy in (0, 1):
            @pl.when(has_y[dy])
            def _():
                edge(t, dy).wait_send()
        for dx in (0, 1):
            for dy in (0, 1):
                @pl.when(has_x[dx] & has_y[dy])
                def _():
                    corner(t, dx, dy).wait_send()
    for x in range(nx):
        far(x).wait_send()
        for way in (0, 1):
            near(x, way).wait_send()
    out_copy.wait()
    for copy in grad_copies:
        copy.wait()


def on_device(
    adjoint_now,
    adjoint_before,
    forward_field,
    velocity,
    thomsen_eps,
    thomsen_delta,
    tilt_level,
    azimuth_level,
    channel_cell,
    channel_count,
    residual_trace,
):
    nx, ny, depth = velocity.shape
    nzb = depth // LANES
    steps = forward_field.shape[0]
    channels = channel_cell.shape[1]
    size_x, size_y, size_s = (lax.axis_size(name) for name in ("gx", "gy", "src"))
    block = jax.ShapeDtypeStruct((nx, ny, LANES), F32)
    anywhere = pl.BlockSpec(memory_space=pl.ANY)
    dma = pltpu.SemaphoreType.DMA
    return pl.pallas_call(
        functools.partial(kernel, size_x, size_y, size_s, ny * size_y),
        name="adjoint_steps",
        out_shape=(jax.ShapeDtypeStruct(adjoint_now.shape, F32), block, block, block),
        in_specs=[anywhere] * 9 + [pl.BlockSpec(memory_space=pltpu.SMEM), anywhere],
        out_specs=(anywhere,) * 4,
        scratch_shapes=[
            pltpu.VMEM((steps, nzb, 2, nx + 2, ny + 2 * TOP, LANES), F32),
            pltpu.VMEM((2, nx, ny, depth), F32),
            pltpu.VMEM((steps, 2, nx, ny, depth), BF16),
            pltpu.VMEM((3, nx, ny, depth), F32),
            pltpu.VMEM((2, nx, ny, depth), jnp.int32),
            pltpu.VMEM((3, nx, ny, LANES), F32),
            pltpu.VMEM((1, channels), jnp.int32),
            pltpu.VMEM((steps, channels), F32),
            pltpu.VMEM((LANES, channels), F32),
            pltpu.VMEM((9, nx, nzb, ny, LANES), F32),
            pltpu.VMEM((steps, nx * ny, LANES), F32),
            pltpu.VMEM((2, nx, nzb, ny, LANES), F32),
            pltpu.VMEM((nzb, 3, nx, ny, LANES), F32),
            pltpu.VMEM((steps, 2, nx, 2 * nzb, LANES), F32),
            pltpu.VMEM((steps, 2, nx, 2 * nzb, LANES), F32),
            pltpu.VMEM((steps, 2, 2, 2 * nzb, LANES), F32),
            pltpu.VMEM((nx, 3, ny, LANES), F32),
            pltpu.VMEM((2, nx, 3, ny, LANES), F32),
            pltpu.VMEM((2, nx, ny, depth), F32),
            pltpu.VMEM((3, nx, ny, LANES), F32),
            dma((nzb + 12,)),
            dma((4,)),
            dma((steps, 2)),
            dma((steps, 2)),
            dma((steps, 2)),
            dma((steps, 2)),
            dma((steps, 2, 2)),
            dma((steps, 2, 2)),
            dma((nx,)),
            dma((nx,)),
            dma((2, nx)),
            dma((2, nx)),
        ],
        compiler_params=pltpu.CompilerParams(
            collective_id=0, has_side_effects=True, vmem_limit_bytes=48 * 1024 * 1024
        ),
    )(
        adjoint_now,
        adjoint_before,
        forward_field,
        velocity,
        thomsen_eps,
        thomsen_delta,
        tilt_level,
        azimuth_level,
        channel_cell,
        channel_count,
        residual_trace,
    )


def solution(mesh):
    placed = (
        P("src", None, "gx", "gy", None),
        P("src", None, "gx", "gy", None),
        P(None, "src", None, "gx", "gy", None),
        P("gx", "gy", None),
        P("gx", "gy", None),
        P("gx", "gy", None),
        P("gx", "gy", None),
        P("gx", "gy", None),
        P("src", None),
        P("src"),
        P("src", None, None),
    )
    return jax.shard_map(
        on_device,
        mesh=mesh,
        in_specs=placed,
        out_specs=(
            P("src", None, "gx", "gy", None),
            P("gx", "gy", "src"),
            P("gx", "gy", "src"),
            P("gx", "gy", "src"),
        ),
        check_vma=False,
    )
```

```python
import functools
import math

import jax
import jax.numpy as jnp
from jax import lax
from jax.experimental import pallas as pl
from jax.experimental.pallas import tpu as pltpu
from jax.sharding import PartitionSpec as P

LEVELS = 32
LANES = 128
ROWS = 8
TOP = 8
MESH = pl.DeviceIdType.MESH
CROSS, CHIP = 0, 1
F32 = jnp.float32
BF16 = jnp.bfloat16


def sin_cos_small(angle):
    sq = angle * angle
    sin = angle + angle * sq * (-1.0 / 6 + sq * (1.0 / 120 + sq * (-1.0 / 5040 + sq * (1.0 / 362880))))
    cos = 1.0 + sq * (-0.5 + sq * (1.0 / 24 + sq * (-1.0 / 720 + sq * (1.0 / 40320 - sq * (1.0 / 3628800)))))
    return sin, cos


def kernel(
    size_x,
    size_y,
    size_s,
    width_y,
    now_hbm,
    before_hbm,
    forward_hbm,
    vel_hbm,
    eps_hbm,
    delta_hbm,
    tilt_hbm,
    azimuth_hbm,
    cell_hbm,
    count_ref,
    trace_hbm,
    next_hbm,
    gvel_hbm,
    geps_hbm,
    gdelta_hbm,
    field,
    before,
    forward,
    params,
    levels,
    own,
    cells,
    traces,
    parts,
    coef,
    surf,
    ha,
    sums,
    edge_out,
    edge_in,
    corner_in,
    far_in,
    near_in,
    result,
    grads,
    load_sem,
    out_sem,
    xs,
    xr,
    ys,
    yr,
    cs,
    cr,
    fs,
    fr,
    ns,
    nr,
):
    gx, gy, me = lax.axis_index("gx"), lax.axis_index("gy"), lax.axis_index("src")
    steps = 3
    nx = now_hbm.shape[2]
    ny = now_hbm.shape[3]
    nzb = now_hbm.shape[4] // LANES
    tiles = ny // ROWS
    body = pl.ds(TOP, ny)
    even = lax.rem(gx, 2) == 0
    below, above = gx > 0, gx < size_x - 1
    has_x = (even & below | ~even & above, even & above | ~even & below)
    sign = jnp.where(even, 1, -1)
    to_x = (gx - sign, gx + sign)
    rim = (jnp.where(even, 0, nx - 1), jnp.where(even, nx - 1, 0))
    halo = (jnp.where(even, 0, nx + 1), jnp.where(even, nx + 1, 0))
    landing = (halo[1], halo[0])
    early = jnp.where(even, 1, 0)
    has_y = (gy > 0, gy < size_y - 1)
    to_y = (gy - 1, gy + 1)
    up = lax.rem(me + 1, size_s)
    down = lax.rem(me + size_s - 1, size_s)
    across = lax.rem(me + 2, size_s)

    def lanes_of(zb):
        return pl.ds(zb * LANES, LANES)

    loads = {}

    def load(name, index, src, dst):
        loads.setdefault(name, []).append(pltpu.make_async_copy(src, dst, load_sem.at[index]))

    for zb in range(nzb):
        load("now", zb, now_hbm.at[0, :, :, :, lanes_of(zb)], field.at[0, zb, :, pl.ds(1, nx), body, :])
    load("angle", nzb, tilt_hbm, levels.at[0])
    load("angle", nzb + 1, azimuth_hbm, levels.at[1])
    load("params", nzb + 2, vel_hbm, params.at[0])
    load("params", nzb + 3, eps_hbm, params.at[1])
    load("params", nzb + 4, delta_hbm, params.at[2])
    load("channels", nzb + 5, cell_hbm, cells)
    load("channels", nzb + 6, trace_hbm.at[:, 0], traces)
    load("before", nzb + 7, before_hbm.at[0], before)
    load("forward", nzb + 8, forward_hbm.at[:, 0], forward)
    mine = pl.ds(pl.multiple_of(me * LANES, LANES), LANES)
    load("own", nzb + 9, vel_hbm.at[:, :, mine], own.at[0])
    load("own", nzb + 10, eps_hbm.at[:, :, mine], own.at[1])
    load("own", nzb + 11, delta_hbm.at[:, :, mine], own.at[2])
    for group in loads.values():
        for copy in group:
            copy.start()

    def arrived(name):
        for copy in loads[name]:
            copy.wait()

    barrier = pltpu.get_barrier_semaphore()
    greeted = jnp.int32(2)
    for side in (CROSS, CHIP):
        @pl.when(has_x[side])
        def _():
            pl.semaphore_signal(barrier, inc=1, device_id={"gx": to_x[side]}, device_id_type=MESH)
        greeted = greeted + has_x[side].astype(jnp.int32)
    for dy in (0, 1):
        @pl.when(has_y[dy])
        def _():
            pl.semaphore_signal(barrier, inc=1, device_id={"gy": to_y[dy]}, device_id_type=MESH)
        greeted = greeted + has_y[dy].astype(jnp.int32)
    for side in (CROSS, CHIP):
        for dy in (0, 1):
            both = has_x[side] & has_y[dy]
            @pl.when(both)
            def _():
                pl.semaphore_signal(
                    barrier, inc=1, device_id={"gx": to_x[side], "gy": to_y[dy]}, device_id_type=MESH
                )
            greeted = greeted + both.astype(jnp.int32)
    for peer in (up, down):
        pl.semaphore_signal(barrier, inc=1, device_id={"src": peer}, device_id_type=MESH)

    for side in (CROSS, CHIP):
        @pl.when(jnp.logical_not(has_x[side]))
        def _():
            zeros = jnp.zeros((ny + 2 * TOP, LANES), F32)
            @pl.loop(0, steps)
            def _(t):
                for zb in range(nzb):
                    for c in (0, 1):
                        field[t, zb, c, halo[side]] = zeros
    for dy in (0, 1):
        @pl.when(jnp.logical_not(has_y[dy]))
        def _():
            row = (TOP - 1, TOP + ny)[dy]
            zeros = jnp.zeros((1, LANES), F32)
            @pl.loop(0, steps)
            def _(t):
                for zb in range(nzb):
                    for c in (0, 1):
                        for x in range(nx + 2):
                            field[t, zb, c, x, pl.ds(row, 1)] = zeros

    def face(t, side):
        return pltpu.make_async_remote_copy(
            src_ref=field.at[t, :, :, rim[side] + 1, body, :],
            dst_ref=field.at[t, :, :, landing[side], body, :],
            send_sem=xs.at[t, side],
            recv_sem=xr.at[t, side],
            device_id={"gx": to_x[side]},
            device_id_type=MESH,
        )

    def first_face(zb, side):
        return pltpu.make_async_remote_copy(
            src_ref=now_hbm.at[0, :, rim[side], :, lanes_of(zb)],
            dst_ref=field.at[0, zb, :, landing[side], body, :],
            send_sem=xs.at[0, side],
            recv_sem=xr.at[0, side],
            device_id={"gx": to_x[side]},
            device_id_type=MESH,
        )

    def planes_of(group):
        return pl.ds(rim[CROSS], 1) if group == CROSS else pl.ds(early, nx - 1)

    def edge(t, dy, group):
        return pltpu.make_async_remote_copy(
            src_ref=edge_out.at[t, dy, planes_of(group)],
            dst_ref=edge_in.at[t, dy, planes_of(group)],
            send_sem=ys.at[t, dy, group],
            recv_sem=yr.at[t, dy, group],
            device_id={"gy": to_y[dy]},
            device_id_type=MESH,
        )

    def corner(t, side, dy):
        return pltpu.make_async_remote_copy(
            src_ref=edge_out.at[t, dy, rim[side]],
            dst_ref=corner_in.at[t, side, dy],
            send_sem=cs.at[t, side, dy],
            recv_sem=cr.at[t, side, dy],
            device_id={"gx": to_x[side], "gy": to_y[dy]},
            device_id_type=MESH,
        )

    def send_face(t, side):
        @pl.when(has_x[side])
        def _():
            face(t, side).start()

    def stage_edges(t, planes):
        for x in planes:
            for zb in range(nzb):
                for c in (0, 1):
                    slot = pl.ds(zb * 2 + c, 1)
                    edge_out[t, 0, x, slot] = field[t, zb, c, x + 1, pl.ds(TOP, 1)]
                    edge_out[t, 1, x, slot] = field[t, zb, c, x + 1, pl.ds(TOP + ny - 1, 1)]

    def send_edges(t, group):
        for dy in (0, 1):
            @pl.when(has_y[dy])
            def _():
                edge(t, dy, group).start()
        for dy in (0, 1):
            @pl.when(has_x[group] & has_y[dy])
            def _():
                corner(t, group, dy).start()

    def receive_edges(t, group):
        planes = (rim[CROSS],) if group == CROSS else tuple(early + i for i in range(nx - 1))
        for dy in (0, 1):
            @pl.when(has_y[1 - dy])
            def _():
                edge(t, dy, group).wait_recv()
                row = (TOP + ny, TOP - 1)[dy]
                for x in planes:
                    for zb in range(nzb):
                        for c in (0, 1):
                            field[t, zb, c, x + 1, pl.ds(row, 1)] = edge_in[t, dy, x, pl.ds(zb * 2 + c, 1)]

    def receive_face(t, side):
        for dy in (0, 1):
            @pl.when(has_x[side] & has_y[1 - dy])
            def _():
                corner(t, side, dy).wait_recv()
                row = (TOP + ny, TOP - 1)[dy]
                for zb in range(nzb):
                    for c in (0, 1):
                        field[t, zb, c, halo[side], pl.ds(row, 1)] = corner_in[
                            t, side, dy, pl.ds(zb * 2 + c, 1)
                        ]
        @pl.when(has_x[side])
        def _():
            face(t, side).wait_recv()

    pl.semaphore_wait(barrier, greeted)
    for side in (CROSS, CHIP):
        @pl.when(has_x[side])
        def _():
            for zb in range(nzb):
                first_face(zb, side).start()
    arrived("now")
    stage_edges(0, range(nx))
    for group in (CHIP, CROSS):
        send_edges(0, group)

    arrived("angle")
    arrived("params")

    @pl.loop(0, nx)
    def _(x):
        for tile in range(tiles):
            rows = pl.ds(tile * ROWS, ROWS)
            for zb in range(nzb):
                cols = lanes_of(zb)
                tilt = levels[0, x, rows, cols].astype(F32)
                turn = levels[1, x, rows, cols].astype(F32)
                sin_h, cos_h = sin_cos_small(tilt * (0.5 * math.pi / LEVELS) - 0.25 * math.pi)
                sin_t = (sin_h + cos_h) * math.sqrt(0.5)
                cos_t = (cos_h - sin_h) * math.sqrt(0.5)
                sin_q, cos_q = sin_cos_small(turn * (0.5 * math.pi / LEVELS) - 0.25 * math.pi)
                sin_2, cos_2 = 2.0 * sin_q * cos_q, 1.0 - 2.0 * sin_q * sin_q
                sin_p, cos_p = -2.0 * sin_2 * cos_2, 2.0 * sin_2 * sin_2 - 1.0
                flat = sin_t * sin_t
                slope = 0.5 * sin_t * cos_t
                coef[0, x, zb, rows] = flat * cos_p * cos_p
                coef[1, x, zb, rows] = flat * sin_p * sin_p
                coef[2, x, zb, rows] = cos_t * cos_t
                coef[3, x, zb, rows] = 0.5 * flat * sin_p * cos_p
                coef[4, x, zb, rows] = slope * sin_p
                coef[5, x, zb, rows] = slope * cos_p
                vel = params[0, x, rows, cols]
                coef[6, x, zb, rows] = vel * vel
                coef[7, x, zb, rows] = 1.0 + 2.0 * params[1, x, rows, cols]
                coef[8, x, zb, rows] = jnp.sqrt(1.0 + 2.0 * params[2, x, rows, cols])

    arrived("channels")
    cell = cells[...]
    local_x = cell // width_y - gx * nx
    local_y = cell % width_y - gy * ny
    slots = lax.broadcasted_iota(jnp.int32, cell.shape, 1)
    inside = (local_x >= 0) & (local_x < nx) & (local_y >= 0) & (local_y < ny) & (slots < count_ref[0])
    target = jnp.where(inside, local_x * ny + local_y, -1)
    spots = lax.broadcasted_iota(jnp.int32, (nx * ny, cell.shape[1]), 0)
    onehot = jnp.where(target == spots, 1.0, 0.0).astype(BF16)
    value = traces[...]
    high = value.astype(BF16).astype(F32)
    middle = (value - high).astype(BF16).astype(F32)
    low = (value - high) - middle
    parts[...] = jnp.zeros_like(parts)
    parts[pl.ds(0, steps)] = high
    parts[pl.ds(steps, steps)] = middle
    parts[pl.ds(2 * steps, steps)] = low
    table = lax.dot_general(
        onehot, parts[...].astype(BF16), (((1,), (1,)), ((), ())), preferred_element_type=F32
    )
    table = table + pltpu.roll(table, LANES - steps, 1) + pltpu.roll(table, LANES - 2 * steps, 1)
    spot_lane = lax.broadcasted_iota(jnp.int32, table.shape, 1)
    for t in range(steps):
        moved = table if t == 0 else pltpu.roll(table, LANES - t, 1)
        surf[t] = jnp.where(spot_lane == 0, moved, 0.0)

    lane = lax.broadcasted_iota(jnp.int32, (ROWS, LANES), 1)
    first, last = lane == 0, lane == LANES - 1
    zero = jnp.zeros((ROWS, LANES), F32)

    def shifted(blocks):
        ahead = [pltpu.roll(block, LANES - 1, 1) for block in blocks] + [zero]
        behind = [zero] + [pltpu.roll(block, 1, 1) for block in blocks]
        after = [jnp.where(last, ahead[i + 1], ahead[i]) for i in range(nzb)]
        prior = [jnp.where(first, behind[i], behind[i + 1]) for i in range(nzb)]
        return after, prior

    def stencil(t, c, x, tile, weights):
        def read(dx, dy):
            rows = pl.ds(TOP + tile * ROWS + dy, ROWS)
            return [field[t, zb, c, x + 1 + dx, rows] for zb in range(nzb)]

        center, right, left, north, south = read(0, 0), read(1, 0), read(-1, 0), read(0, 1), read(0, -1)
        slope_y = [a - b for a, b in zip(north, south)]
        slope_x = [a - b for a, b in zip(right, left)]
        cross = [(a - b) - (d - e) for a, b, d, e in zip(read(1, 1), read(1, -1), read(-1, 1), read(-1, -1))]
        after, prior = shifted(center)
        after_y, prior_y = shifted(slope_y)
        after_x, prior_x = shifted(slope_x)
        out = []
        for zb in range(nzb):
            w = weights[zb]
            sum_x = right[zb] + left[zb]
            sum_y = north[zb] + south[zb]
            sum_z = after[zb] + prior[zb]
            mixed = (
                w[0] * sum_x
                + w[1] * sum_y
                + w[2] * sum_z
                + w[3] * cross[zb]
                + w[4] * (after_y[zb] - prior_y[zb])
                + w[5] * (after_x[zb] - prior_x[zb])
            )
            twice = center[zb] + center[zb]
            if c == 0:
                out.append((sum_x + sum_y + sum_z) - (twice + twice) - mixed)
            else:
                out.append(mixed - twice)
        return out

    def advance(t, x, tile):
        rows = pl.ds(tile * ROWS, ROWS)
        for zb in range(nzb):
            cols = lanes_of(zb)
            horiz, axial = ha[0, x, zb, rows], ha[1, x, zb, rows]
            speed, stretch, root = (coef[i, x, zb, rows] for i in (6, 7, 8))
            updates = (stretch * horiz + root * axial, root * horiz + axial)
            for c in (0, 1):
                here = pl.ds(TOP + tile * ROWS, ROWS)
                center = field[t, zb, c, x + 1, here]
                old = before[c, x, rows, cols] if t == 0 else field[t - 1, zb, c, x + 1, here]
                following = (center + center) - old + speed * updates[c]
                if zb == 0 and c == 0:
                    start = pl.multiple_of(x * ny + tile * ROWS, ROWS)
                    following = following + surf[t, pl.ds(start, ROWS)]
                if t == steps - 1:
                    result[c, x, rows, cols] = following
                else:
                    field[t + 1, zb, c, x + 1, here] = following

    def operators(t, x):
        for tile in range(tiles):
            rows = pl.ds(tile * ROWS, ROWS)
            weights = [[coef[i, x, zb, rows] for i in range(6)] for zb in range(nzb)]
            for c in (0, 1):
                out = stencil(t, c, x, tile, weights)
                for zb in range(nzb):
                    ha[c, x, zb, rows] = out[zb]
            if t < steps - 1:
                advance(t, x, tile)

    def accumulate(t, x):
        for half in range(ny // 16):
            rows = pl.ds(half * 16, 16)
            for zb in range(nzb):
                cols = lanes_of(zb)
                horiz, axial = ha[0, x, zb, rows], ha[1, x, zb, rows]
                pf = forward[t, 0, x, rows, cols].astype(F32)
                qf = forward[t, 1, x, rows, cols].astype(F32)
                terms = (pf * horiz, pf * axial + qf * horiz, qf * axial)
                for i in range(3):
                    sums[zb, i, x, rows] = terms[i] if t == 0 else sums[zb, i, x, rows] + terms[i]

    half = nx // 2

    def onward(x):
        return jnp.where(x < half, up, down)

    def back(x):
        return jnp.where(x < half, down, up)

    def far(x):
        return pltpu.make_async_remote_copy(
            src_ref=sums.at[across, :, x],
            dst_ref=far_in.at[x],
            send_sem=fs.at[x],
            recv_sem=fr.at[x],
            device_id={"src": onward(x)},
            device_id_type=MESH,
        )

    def near(x, peer, slot):
        return pltpu.make_async_remote_copy(
            src_ref=sums.at[peer, :, x],
            dst_ref=near_in.at[slot, x],
            send_sem=ns.at[slot, x],
            recv_sem=nr.at[slot, x],
            device_id={"src": peer},
            device_id_type=MESH,
        )

    def joined(x):
        return near(x, onward(x), 0)

    def single(x):
        return near(x, back(x), 1)

    order = [rim[CHIP] - sign * i for i in range(nx)]
    arrived("before")
    for t in range(steps):
        final = t == steps - 1

        def plane(x):
            operators(t, x)
            if final:
                accumulate(t, x)
                far(x).start()
                single(x).start()

        receive_edges(t, CHIP)
        receive_face(t, CHIP)

        @pl.loop(0, nx - 2)
        def _(i):
            plane(rim[CHIP] - sign * i)

        receive_edges(t, CROSS)
        plane(order[nx - 2])
        if not final:
            send_face(t + 1, CHIP)
            stage_edges(t + 1, order[: nx - 1])
            send_edges(t + 1, CHIP)
        receive_face(t, CROSS)
        plane(order[nx - 1])
        if not final:
            send_face(t + 1, CROSS)
            stage_edges(t + 1, order[nx - 1 :])
            send_edges(t + 1, CROSS)
            if t == 0:
                arrived("forward")

            @pl.loop(0, nx)
            def _(x):
                accumulate(t, x)

    @pl.loop(0, nx)
    def _(x):
        for tile in range(tiles):
            advance(steps - 1, x, tile)

    out_copy = pltpu.make_async_copy(result, next_hbm.at[0], out_sem.at[0])
    out_copy.start()
    for x in order:
        far(x).wait_recv()
        for i in range(3):
            sums[onward(x), i, x] = sums[onward(x), i, x] + far_in[x, i]
        joined(x).start()

    arrived("own")
    for x in order:
        single(x).wait_recv()
        joined(x).wait_recv()
        for tile in range(tiles):
            rows = pl.ds(tile * ROWS, ROWS)
            a, b, c = (
                sums[me, i, x, rows] + near_in[0, x, i, rows] + near_in[1, x, i, rows] for i in range(3)
            )
            vel = own[0, x, rows]
            stretch = 1.0 + 2.0 * own[1, x, rows]
            root = jnp.sqrt(1.0 + 2.0 * own[2, x, rows])
            speed = vel * vel
            grads[0, x, rows] = 2.0 * vel * (stretch * a + root * b + c)
            grads[1, x, rows] = 2.0 * speed * a
            grads[2, x, rows] = speed / root * b
    grad_copies = [
        pltpu.make_async_copy(grads.at[i], out, out_sem.at[1 + i])
        for i, out in enumerate((gvel_hbm, geps_hbm, gdelta_hbm))
    ]
    for copy in grad_copies:
        copy.start()

    for t in range(steps):
        for side in (CROSS, CHIP):
            @pl.when(has_x[side])
            def _():
                face(t, side).wait_send()
        for dy in (0, 1):
            @pl.when(has_y[dy])
            def _():
                for group in (CROSS, CHIP):
                    edge(t, dy, group).wait_send()
            for side in (CROSS, CHIP):
                @pl.when(has_x[side] & has_y[dy])
                def _():
                    corner(t, side, dy).wait_send()
    for x in range(nx):
        far(x).wait_send()
        joined(x).wait_send()
        single(x).wait_send()
    out_copy.wait()
    for copy in grad_copies:
        copy.wait()


def copy_kernel(*refs):
    count = (len(refs) - 1) // 2
    copies = [pltpu.make_async_copy(refs[i], refs[count + i], refs[-1].at[i]) for i in range(count)]
    for copy in copies:
        copy.start()
    for copy in copies:
        copy.wait()


def hand_out(results):
    anywhere = pl.BlockSpec(memory_space=pl.ANY)
    return pl.pallas_call(
        copy_kernel,
        name="hand_out",
        out_shape=tuple(jax.ShapeDtypeStruct(r.shape, r.dtype) for r in results),
        in_specs=[anywhere] * len(results),
        out_specs=(anywhere,) * len(results),
        scratch_shapes=[pltpu.SemaphoreType.DMA((len(results),))],
        compiler_params=pltpu.CompilerParams(vmem_limit_bytes=60 * 1024 * 1024),
    )(*results)


def on_device(
    adjoint_now,
    adjoint_before,
    forward_field,
    velocity,
    thomsen_eps,
    thomsen_delta,
    tilt_level,
    azimuth_level,
    channel_cell,
    channel_count,
    residual_trace,
):
    nx, ny, depth = velocity.shape
    nzb = depth // LANES
    steps = forward_field.shape[0]
    channels = channel_cell.shape[1]
    size_x, size_y, size_s = (lax.axis_size(name) for name in ("gx", "gy", "src"))
    block = jax.ShapeDtypeStruct((nx, ny, LANES), F32)
    anywhere = pl.BlockSpec(memory_space=pl.ANY)
    dma = pltpu.SemaphoreType.DMA
    results = pl.pallas_call(
        functools.partial(kernel, size_x, size_y, size_s, ny * size_y),
        name="adjoint_steps",
        out_shape=(jax.ShapeDtypeStruct(adjoint_now.shape, F32), block, block, block),
        in_specs=[anywhere] * 9 + [pl.BlockSpec(memory_space=pltpu.SMEM), anywhere],
        out_specs=(anywhere,) * 4,
        scratch_shapes=[
            pltpu.VMEM((steps, nzb, 2, nx + 2, ny + 2 * TOP, LANES), F32),
            pltpu.VMEM((2, nx, ny, depth), F32),
            pltpu.VMEM((steps, 2, nx, ny, depth), BF16),
            pltpu.VMEM((3, nx, ny, depth), F32),
            pltpu.VMEM((2, nx, ny, depth), jnp.int32),
            pltpu.VMEM((3, nx, ny, LANES), F32),
            pltpu.VMEM((1, channels), jnp.int32),
            pltpu.VMEM((steps, channels), F32),
            pltpu.VMEM((LANES, channels), F32),
            pltpu.VMEM((9, nx, nzb, ny, LANES), F32),
            pltpu.VMEM((steps, nx * ny, LANES), F32),
            pltpu.VMEM((2, nx, nzb, ny, LANES), F32),
            pltpu.VMEM((nzb, 3, nx, ny, LANES), F32),
            pltpu.VMEM((steps, 2, nx, 2 * nzb, LANES), F32),
            pltpu.VMEM((steps, 2, nx, 2 * nzb, LANES), F32),
            pltpu.VMEM((steps, 2, 2, 2 * nzb, LANES), F32),
            pltpu.VMEM((nx, 3, ny, LANES), F32),
            pltpu.VMEM((2, nx, 3, ny, LANES), F32),
            pltpu.VMEM((2, nx, ny, depth), F32),
            pltpu.VMEM((3, nx, ny, LANES), F32),
            dma((nzb + 12,)),
            dma((4,)),
            dma((steps, 2)),
            dma((steps, 2)),
            dma((steps, 2, 2)),
            dma((steps, 2, 2)),
            dma((steps, 2, 2)),
            dma((steps, 2, 2)),
            dma((nx,)),
            dma((nx,)),
            dma((2, nx)),
            dma((2, nx)),
        ],
        compiler_params=pltpu.CompilerParams(
            collective_id=0, has_side_effects=True, vmem_limit_bytes=60 * 1024 * 1024
        ),
    )(
        adjoint_now,
        adjoint_before,
        forward_field,
        velocity,
        thomsen_eps,
        thomsen_delta,
        tilt_level,
        azimuth_level,
        channel_cell,
        channel_count,
        jnp.transpose(residual_trace, (1, 0, 2)),
    )
    return hand_out(results)


def solution(mesh):
    placed = (
        P("src", None, "gx", "gy", None),
        P("src", None, "gx", "gy", None),
        P(None, "src", None, "gx", "gy", None),
        P("gx", "gy", None),
        P("gx", "gy", None),
        P("gx", "gy", None),
        P("gx", "gy", None),
        P("gx", "gy", None),
        P("src", None),
        P("src"),
        P("src", None, None),
    )
    return jax.shard_map(
        on_device,
        mesh=mesh,
        in_specs=placed,
        out_specs=(
            P("src", None, "gx", "gy", None),
            P("gx", "gy", "src"),
            P("gx", "gy", "src"),
            P("gx", "gy", "src"),
        ),
        check_vma=False,
    )
```

```python
import functools
import math

import jax
import jax.numpy as jnp
from jax import lax
from jax.experimental import pallas as pl
from jax.experimental.pallas import tpu as pltpu
from jax.sharding import PartitionSpec as P

LEVELS = 32
LANES = 128
ROWS = 8
TOP = 8
MESH = pl.DeviceIdType.MESH
CROSS, CHIP = 0, 1
F32 = jnp.float32
BF16 = jnp.bfloat16


def sin_cos_small(angle):
    sq = angle * angle
    sin = angle + angle * sq * (-1.0 / 6 + sq * (1.0 / 120 + sq * (-1.0 / 5040 + sq * (1.0 / 362880))))
    cos = 1.0 + sq * (-0.5 + sq * (1.0 / 24 + sq * (-1.0 / 720 + sq * (1.0 / 40320 - sq * (1.0 / 3628800)))))
    return sin, cos


def kernel(
    size_x,
    size_y,
    size_s,
    width_y,
    now_hbm,
    before_hbm,
    forward_hbm,
    vel_hbm,
    eps_hbm,
    delta_hbm,
    tilt_hbm,
    azimuth_hbm,
    cell_hbm,
    count_ref,
    trace_hbm,
    next_hbm,
    gvel_hbm,
    geps_hbm,
    gdelta_hbm,
    field,
    before,
    forward,
    params,
    levels,
    own,
    cells,
    traces,
    parts,
    coef,
    surf,
    ha,
    sums,
    edge_out,
    edge_in,
    corner_in,
    far_in,
    near_in,
    result,
    grads,
    load_sem,
    out_sem,
    xs,
    xr,
    ys,
    yr,
    cs,
    cr,
    fs,
    fr,
    ns,
    nr,
):
    gx, gy, me = lax.axis_index("gx"), lax.axis_index("gy"), lax.axis_index("src")
    steps = 3
    nx = now_hbm.shape[2]
    ny = now_hbm.shape[3]
    nzb = now_hbm.shape[4] // LANES
    tiles = ny // ROWS
    body = pl.ds(TOP, ny)
    even = lax.rem(gx, 2) == 0
    below, above = gx > 0, gx < size_x - 1
    has_x = (even & below | ~even & above, even & above | ~even & below)
    sign = jnp.where(even, 1, -1)
    to_x = (gx - sign, gx + sign)
    rim = (jnp.where(even, 0, nx - 1), jnp.where(even, nx - 1, 0))
    halo = (jnp.where(even, 0, nx + 1), jnp.where(even, nx + 1, 0))
    landing = (halo[1], halo[0])
    early = jnp.where(even, 1, 0)
    has_y = (gy > 0, gy < size_y - 1)
    to_y = (gy - 1, gy + 1)
    up = lax.rem(me + 1, size_s)
    down = lax.rem(me + size_s - 1, size_s)
    across = lax.rem(me + 2, size_s)

    def lanes_of(zb):
        return pl.ds(zb * LANES, LANES)

    loads = {}

    def load(name, index, src, dst):
        loads.setdefault(name, []).append(pltpu.make_async_copy(src, dst, load_sem.at[index]))

    for zb in range(nzb):
        load("now", zb, now_hbm.at[0, :, :, :, lanes_of(zb)], field.at[0, zb, :, pl.ds(1, nx), body, :])
    load("angle", nzb, tilt_hbm, levels.at[0])
    load("angle", nzb + 1, azimuth_hbm, levels.at[1])
    load("params", nzb + 2, vel_hbm, params.at[0])
    load("params", nzb + 3, eps_hbm, params.at[1])
    load("params", nzb + 4, delta_hbm, params.at[2])
    load("channels", nzb + 5, cell_hbm, cells)
    load("channels", nzb + 6, trace_hbm.at[:, 0], traces)
    load("before", nzb + 7, before_hbm.at[0], before)
    load("forward", nzb + 8, forward_hbm.at[:, 0], forward)
    mine = pl.ds(pl.multiple_of(me * LANES, LANES), LANES)
    load("own", nzb + 9, vel_hbm.at[:, :, mine], own.at[0])
    load("own", nzb + 10, eps_hbm.at[:, :, mine], own.at[1])
    load("own", nzb + 11, delta_hbm.at[:, :, mine], own.at[2])
    for group in loads.values():
        for copy in group:
            copy.start()

    def arrived(name):
        for copy in loads[name]:
            copy.wait()

    barrier = pltpu.get_barrier_semaphore()
    greeted = jnp.int32(2)
    for side in (CROSS, CHIP):
        @pl.when(has_x[side])
        def _():
            pl.semaphore_signal(barrier, inc=1, device_id={"gx": to_x[side]}, device_id_type=MESH)
        greeted = greeted + has_x[side].astype(jnp.int32)
    for dy in (0, 1):
        @pl.when(has_y[dy])
        def _():
            pl.semaphore_signal(barrier, inc=1, device_id={"gy": to_y[dy]}, device_id_type=MESH)
        greeted = greeted + has_y[dy].astype(jnp.int32)
    for side in (CROSS, CHIP):
        for dy in (0, 1):
            both = has_x[side] & has_y[dy]
            @pl.when(both)
            def _():
                pl.semaphore_signal(
                    barrier, inc=1, device_id={"gx": to_x[side], "gy": to_y[dy]}, device_id_type=MESH
                )
            greeted = greeted + both.astype(jnp.int32)
    for peer in (up, down):
        pl.semaphore_signal(barrier, inc=1, device_id={"src": peer}, device_id_type=MESH)

    for side in (CROSS, CHIP):
        @pl.when(jnp.logical_not(has_x[side]))
        def _():
            zeros = jnp.zeros((ny + 2 * TOP, LANES), F32)
            @pl.loop(0, steps)
            def _(t):
                for zb in range(nzb):
                    for c in (0, 1):
                        field[t, zb, c, halo[side]] = zeros
    for dy in (0, 1):
        @pl.when(jnp.logical_not(has_y[dy]))
        def _():
            row = (TOP - 1, TOP + ny)[dy]
            zeros = jnp.zeros((1, LANES), F32)
            @pl.loop(0, steps)
            def _(t):
                for zb in range(nzb):
                    for c in (0, 1):
                        for x in range(nx + 2):
                            field[t, zb, c, x, pl.ds(row, 1)] = zeros

    def face(t, side):
        return pltpu.make_async_remote_copy(
            src_ref=field.at[t, :, :, rim[side] + 1, body, :],
            dst_ref=field.at[t, :, :, landing[side], body, :],
            send_sem=xs.at[t, side],
            recv_sem=xr.at[t, side],
            device_id={"gx": to_x[side]},
            device_id_type=MESH,
        )

    def first_face(zb, side):
        return pltpu.make_async_remote_copy(
            src_ref=now_hbm.at[0, :, rim[side], :, lanes_of(zb)],
            dst_ref=field.at[0, zb, :, landing[side], body, :],
            send_sem=xs.at[0, side],
            recv_sem=xr.at[0, side],
            device_id={"gx": to_x[side]},
            device_id_type=MESH,
        )

    def planes_of(group):
        return pl.ds(rim[CROSS], 1) if group == CROSS else pl.ds(early, nx - 1)

    def edge(t, dy, group):
        return pltpu.make_async_remote_copy(
            src_ref=edge_out.at[t, dy, planes_of(group)],
            dst_ref=edge_in.at[t, dy, planes_of(group)],
            send_sem=ys.at[t, dy, group],
            recv_sem=yr.at[t, dy, group],
            device_id={"gy": to_y[dy]},
            device_id_type=MESH,
        )

    def corner(t, side, dy):
        return pltpu.make_async_remote_copy(
            src_ref=edge_out.at[t, dy, rim[side]],
            dst_ref=corner_in.at[t, side, dy],
            send_sem=cs.at[t, side, dy],
            recv_sem=cr.at[t, side, dy],
            device_id={"gx": to_x[side], "gy": to_y[dy]},
            device_id_type=MESH,
        )

    def send_face(t, side):
        @pl.when(has_x[side])
        def _():
            face(t, side).start()

    def stage_edges(t, planes):
        for x in planes:
            for zb in range(nzb):
                for c in (0, 1):
                    slot = pl.ds(zb * 2 + c, 1)
                    edge_out[t, 0, x, slot] = field[t, zb, c, x + 1, pl.ds(TOP, 1)]
                    edge_out[t, 1, x, slot] = field[t, zb, c, x + 1, pl.ds(TOP + ny - 1, 1)]

    def send_edges(t, group):
        for dy in (0, 1):
            @pl.when(has_y[dy])
            def _():
                edge(t, dy, group).start()
        for dy in (0, 1):
            @pl.when(has_x[group] & has_y[dy])
            def _():
                corner(t, group, dy).start()

    def receive_edges(t, group):
        planes = (rim[CROSS],) if group == CROSS else tuple(early + i for i in range(nx - 1))
        for dy in (0, 1):
            @pl.when(has_y[1 - dy])
            def _():
                edge(t, dy, group).wait_recv()
                row = (TOP + ny, TOP - 1)[dy]
                for x in planes:
                    for zb in range(nzb):
                        for c in (0, 1):
                            field[t, zb, c, x + 1, pl.ds(row, 1)] = edge_in[t, dy, x, pl.ds(zb * 2 + c, 1)]

    def receive_face(t, side):
        for dy in (0, 1):
            @pl.when(has_x[side] & has_y[1 - dy])
            def _():
                corner(t, side, dy).wait_recv()
                row = (TOP + ny, TOP - 1)[dy]
                for zb in range(nzb):
                    for c in (0, 1):
                        field[t, zb, c, halo[side], pl.ds(row, 1)] = corner_in[
                            t, side, dy, pl.ds(zb * 2 + c, 1)
                        ]
        @pl.when(has_x[side])
        def _():
            face(t, side).wait_recv()

    pl.semaphore_wait(barrier, greeted)
    for side in (CROSS, CHIP):
        @pl.when(has_x[side])
        def _():
            for zb in range(nzb):
                first_face(zb, side).start()
    arrived("now")
    stage_edges(0, range(nx))
    for group in (CHIP, CROSS):
        send_edges(0, group)

    arrived("angle")
    arrived("params")

    @pl.loop(0, nx)
    def _(x):
        for tile in range(tiles):
            rows = pl.ds(tile * ROWS, ROWS)
            for zb in range(nzb):
                cols = lanes_of(zb)
                tilt = levels[0, x, rows, cols].astype(F32)
                turn = levels[1, x, rows, cols].astype(F32)
                sin_h, cos_h = sin_cos_small(tilt * (0.5 * math.pi / LEVELS) - 0.25 * math.pi)
                sin_t = (sin_h + cos_h) * math.sqrt(0.5)
                cos_t = (cos_h - sin_h) * math.sqrt(0.5)
                sin_q, cos_q = sin_cos_small(turn * (0.5 * math.pi / LEVELS) - 0.25 * math.pi)
                sin_2, cos_2 = 2.0 * sin_q * cos_q, 1.0 - 2.0 * sin_q * sin_q
                sin_p, cos_p = -2.0 * sin_2 * cos_2, 2.0 * sin_2 * sin_2 - 1.0
                flat = sin_t * sin_t
                slope = 0.5 * sin_t * cos_t
                coef[0, x, zb, rows] = flat * cos_p * cos_p
                coef[1, x, zb, rows] = flat * sin_p * sin_p
                coef[2, x, zb, rows] = cos_t * cos_t
                coef[3, x, zb, rows] = 0.5 * flat * sin_p * cos_p
                coef[4, x, zb, rows] = slope * sin_p
                coef[5, x, zb, rows] = slope * cos_p
                vel = params[0, x, rows, cols]
                coef[6, x, zb, rows] = vel * vel
                coef[7, x, zb, rows] = 1.0 + 2.0 * params[1, x, rows, cols]
                coef[8, x, zb, rows] = jnp.sqrt(1.0 + 2.0 * params[2, x, rows, cols])

    arrived("channels")
    cell = cells[...]
    local_x = cell // width_y - gx * nx
    local_y = cell % width_y - gy * ny
    slots = lax.broadcasted_iota(jnp.int32, cell.shape, 1)
    inside = (local_x >= 0) & (local_x < nx) & (local_y >= 0) & (local_y < ny) & (slots < count_ref[0])
    target = jnp.where(inside, local_x * ny + local_y, -1)
    spots = lax.broadcasted_iota(jnp.int32, (nx * ny, cell.shape[1]), 0)
    onehot = jnp.where(target == spots, 1.0, 0.0).astype(BF16)
    value = traces[...]
    high = value.astype(BF16).astype(F32)
    middle = (value - high).astype(BF16).astype(F32)
    low = (value - high) - middle
    parts[...] = jnp.zeros_like(parts)
    parts[pl.ds(0, steps)] = high
    parts[pl.ds(steps, steps)] = middle
    parts[pl.ds(2 * steps, steps)] = low
    table = lax.dot_general(
        onehot, parts[...].astype(BF16), (((1,), (1,)), ((), ())), preferred_element_type=F32
    )
    table = table + pltpu.roll(table, LANES - steps, 1) + pltpu.roll(table, LANES - 2 * steps, 1)
    spot_lane = lax.broadcasted_iota(jnp.int32, table.shape, 1)
    for t in range(steps):
        moved = table if t == 0 else pltpu.roll(table, LANES - t, 1)
        surf[t] = jnp.where(spot_lane == 0, moved, 0.0)

    lane = lax.broadcasted_iota(jnp.int32, (ROWS, LANES), 1)
    first, last = lane == 0, lane == LANES - 1
    zero = jnp.zeros((ROWS, LANES), F32)

    def shifted(blocks):
        ahead = [pltpu.roll(block, LANES - 1, 1) for block in blocks] + [zero]
        behind = [zero] + [pltpu.roll(block, 1, 1) for block in blocks]
        after = [jnp.where(last, ahead[i + 1], ahead[i]) for i in range(nzb)]
        prior = [jnp.where(first, behind[i], behind[i + 1]) for i in range(nzb)]
        return after, prior

    def stencil(t, c, x, tile, weights):
        def read(dx, dy):
            rows = pl.ds(TOP + tile * ROWS + dy, ROWS)
            return [field[t, zb, c, x + 1 + dx, rows] for zb in range(nzb)]

        center, right, left, north, south = read(0, 0), read(1, 0), read(-1, 0), read(0, 1), read(0, -1)
        slope_y = [a - b for a, b in zip(north, south)]
        slope_x = [a - b for a, b in zip(right, left)]
        cross = [(a - b) - (d - e) for a, b, d, e in zip(read(1, 1), read(1, -1), read(-1, 1), read(-1, -1))]
        after, prior = shifted(center)
        after_y, prior_y = shifted(slope_y)
        after_x, prior_x = shifted(slope_x)
        out = []
        for zb in range(nzb):
            w = weights[zb]
            sum_x = right[zb] + left[zb]
            sum_y = north[zb] + south[zb]
            sum_z = after[zb] + prior[zb]
            mixed = (
                w[0] * sum_x
                + w[1] * sum_y
                + w[2] * sum_z
                + w[3] * cross[zb]
                + w[4] * (after_y[zb] - prior_y[zb])
                + w[5] * (after_x[zb] - prior_x[zb])
            )
            twice = center[zb] + center[zb]
            if c == 0:
                out.append((sum_x + sum_y + sum_z) - (twice + twice) - mixed)
            else:
                out.append(mixed - twice)
        return out

    def advance(t, x, tile):
        rows = pl.ds(tile * ROWS, ROWS)
        for zb in range(nzb):
            cols = lanes_of(zb)
            horiz, axial = ha[0, x, zb, rows], ha[1, x, zb, rows]
            speed, stretch, root = (coef[i, x, zb, rows] for i in (6, 7, 8))
            updates = (stretch * horiz + root * axial, root * horiz + axial)
            for c in (0, 1):
                here = pl.ds(TOP + tile * ROWS, ROWS)
                center = field[t, zb, c, x + 1, here]
                old = before[c, x, rows, cols] if t == 0 else field[t - 1, zb, c, x + 1, here]
                following = (center + center) - old + speed * updates[c]
                if zb == 0 and c == 0:
                    start = pl.multiple_of(x * ny + tile * ROWS, ROWS)
                    following = following + surf[t, pl.ds(start, ROWS)]
                if t == steps - 1:
                    result[c, x, rows, cols] = following
                else:
                    field[t + 1, zb, c, x + 1, here] = following

    def operators(t, x):
        for tile in range(tiles):
            rows = pl.ds(tile * ROWS, ROWS)
            weights = [[coef[i, x, zb, rows] for i in range(6)] for zb in range(nzb)]
            for c in (0, 1):
                out = stencil(t, c, x, tile, weights)
                for zb in range(nzb):
                    ha[c, x, zb, rows] = out[zb]
            if t < steps - 1:
                advance(t, x, tile)

    def accumulate(t, x):
        for half in range(ny // 16):
            rows = pl.ds(half * 16, 16)
            for zb in range(nzb):
                cols = lanes_of(zb)
                horiz, axial = ha[0, x, zb, rows], ha[1, x, zb, rows]
                pf = forward[t, 0, x, rows, cols].astype(F32)
                qf = forward[t, 1, x, rows, cols].astype(F32)
                terms = (pf * horiz, pf * axial + qf * horiz, qf * axial)
                for i in range(3):
                    sums[zb, i, x, rows] = terms[i] if t == 0 else sums[zb, i, x, rows] + terms[i]

    half = nx // 2

    def onward(x):
        return jnp.where(x < half, up, down)

    def back(x):
        return jnp.where(x < half, down, up)

    def far(x):
        return pltpu.make_async_remote_copy(
            src_ref=sums.at[across, :, x],
            dst_ref=far_in.at[x],
            send_sem=fs.at[x],
            recv_sem=fr.at[x],
            device_id={"src": onward(x)},
            device_id_type=MESH,
        )

    def near(x, peer, slot):
        return pltpu.make_async_remote_copy(
            src_ref=sums.at[peer, :, x],
            dst_ref=near_in.at[slot, x],
            send_sem=ns.at[slot, x],
            recv_sem=nr.at[slot, x],
            device_id={"src": peer},
            device_id_type=MESH,
        )

    def joined(x):
        return near(x, onward(x), 0)

    def single(x):
        return near(x, back(x), 1)

    order = [rim[CHIP] - sign * i for i in range(nx)]
    arrived("before")
    for t in range(steps):
        final = t == steps - 1

        def plane(x):
            operators(t, x)
            if final:
                accumulate(t, x)
                far(x).start()
                single(x).start()

        receive_edges(t, CHIP)
        receive_face(t, CHIP)

        @pl.loop(0, nx - 2)
        def _(i):
            plane(rim[CHIP] - sign * i)

        receive_edges(t, CROSS)
        plane(order[nx - 2])
        if not final:
            send_face(t + 1, CHIP)
            stage_edges(t + 1, order[: nx - 1])
            send_edges(t + 1, CHIP)
        receive_face(t, CROSS)
        plane(order[nx - 1])
        if not final:
            send_face(t + 1, CROSS)
            stage_edges(t + 1, order[nx - 1 :])
            send_edges(t + 1, CROSS)
            if t == 0:
                arrived("forward")

            @pl.loop(0, nx)
            def _(x):
                accumulate(t, x)

    @pl.loop(0, nx)
    def _(x):
        for tile in range(tiles):
            advance(steps - 1, x, tile)

    out_copy = pltpu.make_async_copy(result, next_hbm.at[0], out_sem.at[0])
    out_copy.start()
    for x in order:
        far(x).wait_recv()
        for i in range(3):
            sums[onward(x), i, x] = sums[onward(x), i, x] + far_in[x, i]
        joined(x).start()

    arrived("own")
    for x in order:
        single(x).wait_recv()
        joined(x).wait_recv()
        for tile in range(tiles):
            rows = pl.ds(tile * ROWS, ROWS)
            a, b, c = (
                sums[me, i, x, rows] + near_in[0, x, i, rows] + near_in[1, x, i, rows] for i in range(3)
            )
            vel = own[0, x, rows]
            stretch = 1.0 + 2.0 * own[1, x, rows]
            root = jnp.sqrt(1.0 + 2.0 * own[2, x, rows])
            speed = vel * vel
            grads[0, x, rows] = 2.0 * vel * (stretch * a + root * b + c)
            grads[1, x, rows] = 2.0 * speed * a
            grads[2, x, rows] = speed / root * b
    grad_copies = [
        pltpu.make_async_copy(grads.at[i], out, out_sem.at[1 + i])
        for i, out in enumerate((gvel_hbm, geps_hbm, gdelta_hbm))
    ]
    for copy in grad_copies:
        copy.start()

    for t in range(steps):
        for side in (CROSS, CHIP):
            @pl.when(has_x[side])
            def _():
                face(t, side).wait_send()
        for dy in (0, 1):
            @pl.when(has_y[dy])
            def _():
                for group in (CROSS, CHIP):
                    edge(t, dy, group).wait_send()
            for side in (CROSS, CHIP):
                @pl.when(has_x[side] & has_y[dy])
                def _():
                    corner(t, side, dy).wait_send()
    for x in range(nx):
        far(x).wait_send()
        joined(x).wait_send()
        single(x).wait_send()
    out_copy.wait()
    for copy in grad_copies:
        copy.wait()


def copy_kernel(*refs):
    sources, targets, stages = refs[:4], refs[4:8], refs[8:12]
    fetched, stored = refs[12:]
    pieces = [(0, (0, c, x)) for c in (0, 1) for x in range(sources[0].shape[2])]
    pieces += [(i, ()) for i in (1, 2, 3)]
    fetches, stores = [], []
    for slot, (i, at) in enumerate(pieces):
        source, stage, target = (ref.at[at] if at else ref for ref in (sources[i], stages[i], targets[i]))
        fetches.append(pltpu.make_async_copy(source, stage, fetched.at[slot]))
        stores.append(pltpu.make_async_copy(stage, target, stored.at[slot]))
    for fetch in fetches:
        fetch.start()
    for fetch, store in zip(fetches, stores):
        fetch.wait()
        store.start()
    for store in stores:
        store.wait()


def hand_out(results):
    anywhere = pl.BlockSpec(memory_space=pl.ANY)
    pieces = 2 * results[0].shape[2] + 3
    return pl.pallas_call(
        copy_kernel,
        name="hand_out",
        out_shape=tuple(jax.ShapeDtypeStruct(r.shape, r.dtype) for r in results),
        in_specs=[anywhere] * len(results),
        out_specs=(anywhere,) * len(results),
        scratch_shapes=[pltpu.VMEM(r.shape, r.dtype) for r in results] + [pltpu.SemaphoreType.DMA((pieces,))] * 2,
        compiler_params=pltpu.CompilerParams(vmem_limit_bytes=60 * 1024 * 1024),
    )(*results)


def on_device(
    adjoint_now,
    adjoint_before,
    forward_field,
    velocity,
    thomsen_eps,
    thomsen_delta,
    tilt_level,
    azimuth_level,
    channel_cell,
    channel_count,
    residual_trace,
):
    nx, ny, depth = velocity.shape
    nzb = depth // LANES
    steps = forward_field.shape[0]
    channels = channel_cell.shape[1]
    size_x, size_y, size_s = (lax.axis_size(name) for name in ("gx", "gy", "src"))
    block = jax.ShapeDtypeStruct((nx, ny, LANES), F32)
    anywhere = pl.BlockSpec(memory_space=pl.ANY)
    dma = pltpu.SemaphoreType.DMA
    results = pl.pallas_call(
        functools.partial(kernel, size_x, size_y, size_s, ny * size_y),
        name="adjoint_steps",
        out_shape=(jax.ShapeDtypeStruct(adjoint_now.shape, F32), block, block, block),
        in_specs=[anywhere] * 9 + [pl.BlockSpec(memory_space=pltpu.SMEM), anywhere],
        out_specs=(anywhere,) * 4,
        scratch_shapes=[
            pltpu.VMEM((steps, nzb, 2, nx + 2, ny + 2 * TOP, LANES), F32),
            pltpu.VMEM((2, nx, ny, depth), F32),
            pltpu.VMEM((steps, 2, nx, ny, depth), BF16),
            pltpu.VMEM((3, nx, ny, depth), F32),
            pltpu.VMEM((2, nx, ny, depth), jnp.int32),
            pltpu.VMEM((3, nx, ny, LANES), F32),
            pltpu.VMEM((1, channels), jnp.int32),
            pltpu.VMEM((steps, channels), F32),
            pltpu.VMEM((LANES, channels), F32),
            pltpu.VMEM((9, nx, nzb, ny, LANES), F32),
            pltpu.VMEM((steps, nx * ny, LANES), F32),
            pltpu.VMEM((2, nx, nzb, ny, LANES), F32),
            pltpu.VMEM((nzb, 3, nx, ny, LANES), F32),
            pltpu.VMEM((steps, 2, nx, 2 * nzb, LANES), F32),
            pltpu.VMEM((steps, 2, nx, 2 * nzb, LANES), F32),
            pltpu.VMEM((steps, 2, 2, 2 * nzb, LANES), F32),
            pltpu.VMEM((nx, 3, ny, LANES), F32),
            pltpu.VMEM((2, nx, 3, ny, LANES), F32),
            pltpu.VMEM((2, nx, ny, depth), F32),
            pltpu.VMEM((3, nx, ny, LANES), F32),
            dma((nzb + 12,)),
            dma((4,)),
            dma((steps, 2)),
            dma((steps, 2)),
            dma((steps, 2, 2)),
            dma((steps, 2, 2)),
            dma((steps, 2, 2)),
            dma((steps, 2, 2)),
            dma((nx,)),
            dma((nx,)),
            dma((2, nx)),
            dma((2, nx)),
        ],
        compiler_params=pltpu.CompilerParams(
            collective_id=0, has_side_effects=True, vmem_limit_bytes=60 * 1024 * 1024
        ),
    )(
        adjoint_now,
        adjoint_before,
        forward_field,
        velocity,
        thomsen_eps,
        thomsen_delta,
        tilt_level,
        azimuth_level,
        channel_cell,
        channel_count,
        jnp.transpose(residual_trace, (1, 0, 2)),
    )
    return hand_out(results)


def solution(mesh):
    placed = (
        P("src", None, "gx", "gy", None),
        P("src", None, "gx", "gy", None),
        P(None, "src", None, "gx", "gy", None),
        P("gx", "gy", None),
        P("gx", "gy", None),
        P("gx", "gy", None),
        P("gx", "gy", None),
        P("gx", "gy", None),
        P("src", None),
        P("src"),
        P("src", None, None),
    )
    return jax.shard_map(
        on_device,
        mesh=mesh,
        in_specs=placed,
        out_specs=(
            P("src", None, "gx", "gy", None),
            P("gx", "gy", "src"),
            P("gx", "gy", "src"),
            P("gx", "gy", "src"),
        ),
        check_vma=False,
    )
```

```python
import functools
import math

import jax
import jax.numpy as jnp
from jax import lax
from jax.experimental import pallas as pl
from jax.experimental.pallas import tpu as pltpu
from jax.sharding import PartitionSpec as P

LEVELS = 32
LANES = 128
ROWS = 8
TOP = 8
MESH = pl.DeviceIdType.MESH
CROSS, CHIP = 0, 1
F32 = jnp.float32
BF16 = jnp.bfloat16


def sin_cos_small(angle):
    sq = angle * angle
    sin = angle + angle * sq * (-1.0 / 6 + sq * (1.0 / 120 + sq * (-1.0 / 5040 + sq * (1.0 / 362880))))
    cos = 1.0 + sq * (-0.5 + sq * (1.0 / 24 + sq * (-1.0 / 720 + sq * (1.0 / 40320 - sq * (1.0 / 3628800)))))
    return sin, cos


def kernel(
    size_x,
    size_y,
    size_s,
    width_y,
    now_hbm,
    before_hbm,
    forward_hbm,
    vel_hbm,
    eps_hbm,
    delta_hbm,
    tilt_hbm,
    azimuth_hbm,
    cell_hbm,
    count_ref,
    trace_hbm,
    next_hbm,
    gvel_hbm,
    geps_hbm,
    gdelta_hbm,
    field,
    before,
    forward,
    wide,
    params,
    levels,
    own,
    cells,
    traces,
    parts,
    coef,
    surf,
    ha,
    sums,
    edge_out,
    edge_in,
    corner_in,
    far_in,
    near_in,
    result,
    grads,
    load_sem,
    out_sem,
    xs,
    xr,
    ys,
    yr,
    cs,
    cr,
    fs,
    fr,
    ns,
    nr,
):
    gx, gy, me = lax.axis_index("gx"), lax.axis_index("gy"), lax.axis_index("src")
    steps = 3
    nx = now_hbm.shape[2]
    ny = now_hbm.shape[3]
    nzb = now_hbm.shape[4] // LANES
    tiles = ny // ROWS
    body = pl.ds(TOP, ny)
    even = lax.rem(gx, 2) == 0
    below, above = gx > 0, gx < size_x - 1
    has_x = (even & below | ~even & above, even & above | ~even & below)
    sign = jnp.where(even, 1, -1)
    to_x = (gx - sign, gx + sign)
    rim = (jnp.where(even, 0, nx - 1), jnp.where(even, nx - 1, 0))
    halo = (jnp.where(even, 0, nx + 1), jnp.where(even, nx + 1, 0))
    landing = (halo[1], halo[0])
    early = jnp.where(even, 1, 0)
    has_y = (gy > 0, gy < size_y - 1)
    to_y = (gy - 1, gy + 1)
    up = lax.rem(me + 1, size_s)
    down = lax.rem(me + size_s - 1, size_s)
    across = lax.rem(me + 2, size_s)

    def lanes_of(zb):
        return pl.ds(zb * LANES, LANES)

    loads = {}

    def load(name, index, src, dst):
        loads.setdefault(name, []).append(pltpu.make_async_copy(src, dst, load_sem.at[index]))

    for zb in range(nzb):
        load("now", zb, now_hbm.at[0, :, :, :, lanes_of(zb)], field.at[0, zb, :, pl.ds(1, nx), body, :])
    load("angle", nzb, tilt_hbm, levels.at[0])
    load("angle", nzb + 1, azimuth_hbm, levels.at[1])
    load("params", nzb + 2, vel_hbm, params.at[0])
    load("params", nzb + 3, eps_hbm, params.at[1])
    load("params", nzb + 4, delta_hbm, params.at[2])
    load("channels", nzb + 5, cell_hbm, cells)
    load("channels", nzb + 6, trace_hbm.at[:, 0], traces)
    load("before", nzb + 7, before_hbm.at[0], before)
    load("forward", nzb + 8, forward_hbm.at[:, 0], forward)
    mine = pl.ds(pl.multiple_of(me * LANES, LANES), LANES)
    load("own", nzb + 9, vel_hbm.at[:, :, mine], own.at[0])
    load("own", nzb + 10, eps_hbm.at[:, :, mine], own.at[1])
    load("own", nzb + 11, delta_hbm.at[:, :, mine], own.at[2])
    for group in loads.values():
        for copy in group:
            copy.start()

    def arrived(name):
        for copy in loads[name]:
            copy.wait()

    barrier = pltpu.get_barrier_semaphore()
    greeted = jnp.int32(2)
    for side in (CROSS, CHIP):
        @pl.when(has_x[side])
        def _():
            pl.semaphore_signal(barrier, inc=1, device_id={"gx": to_x[side]}, device_id_type=MESH)
        greeted = greeted + has_x[side].astype(jnp.int32)
    for dy in (0, 1):
        @pl.when(has_y[dy])
        def _():
            pl.semaphore_signal(barrier, inc=1, device_id={"gy": to_y[dy]}, device_id_type=MESH)
        greeted = greeted + has_y[dy].astype(jnp.int32)
    for side in (CROSS, CHIP):
        for dy in (0, 1):
            both = has_x[side] & has_y[dy]
            @pl.when(both)
            def _():
                pl.semaphore_signal(
                    barrier, inc=1, device_id={"gx": to_x[side], "gy": to_y[dy]}, device_id_type=MESH
                )
            greeted = greeted + both.astype(jnp.int32)
    for peer in (up, down):
        pl.semaphore_signal(barrier, inc=1, device_id={"src": peer}, device_id_type=MESH)

    for side in (CROSS, CHIP):
        @pl.when(jnp.logical_not(has_x[side]))
        def _():
            zeros = jnp.zeros((ny + 2 * TOP, LANES), F32)
            @pl.loop(0, steps)
            def _(t):
                for zb in range(nzb):
                    for c in (0, 1):
                        field[t, zb, c, halo[side]] = zeros
    for dy in (0, 1):
        @pl.when(jnp.logical_not(has_y[dy]))
        def _():
            row = (TOP - 1, TOP + ny)[dy]
            zeros = jnp.zeros((1, LANES), F32)
            @pl.loop(0, steps)
            def _(t):
                for zb in range(nzb):
                    for c in (0, 1):
                        for x in range(nx + 2):
                            field[t, zb, c, x, pl.ds(row, 1)] = zeros

    def face(t, side):
        return pltpu.make_async_remote_copy(
            src_ref=field.at[t, :, :, rim[side] + 1, body, :],
            dst_ref=field.at[t, :, :, landing[side], body, :],
            send_sem=xs.at[t, side],
            recv_sem=xr.at[t, side],
            device_id={"gx": to_x[side]},
            device_id_type=MESH,
        )

    def first_face(zb, side):
        return pltpu.make_async_remote_copy(
            src_ref=now_hbm.at[0, :, rim[side], :, lanes_of(zb)],
            dst_ref=field.at[0, zb, :, landing[side], body, :],
            send_sem=xs.at[0, side],
            recv_sem=xr.at[0, side],
            device_id={"gx": to_x[side]},
            device_id_type=MESH,
        )

    def planes_of(group):
        return pl.ds(rim[CROSS], 1) if group == CROSS else pl.ds(early, nx - 1)

    def edge(t, dy, group):
        return pltpu.make_async_remote_copy(
            src_ref=edge_out.at[t, dy, planes_of(group)],
            dst_ref=edge_in.at[t, dy, planes_of(group)],
            send_sem=ys.at[t, dy, group],
            recv_sem=yr.at[t, dy, group],
            device_id={"gy": to_y[dy]},
            device_id_type=MESH,
        )

    def corner(t, side, dy):
        return pltpu.make_async_remote_copy(
            src_ref=edge_out.at[t, dy, rim[side]],
            dst_ref=corner_in.at[t, side, dy],
            send_sem=cs.at[t, side, dy],
            recv_sem=cr.at[t, side, dy],
            device_id={"gx": to_x[side], "gy": to_y[dy]},
            device_id_type=MESH,
        )

    def send_face(t, side):
        @pl.when(has_x[side])
        def _():
            face(t, side).start()

    def stage_edges(t, planes):
        for x in planes:
            for zb in range(nzb):
                for c in (0, 1):
                    slot = pl.ds(zb * 2 + c, 1)
                    edge_out[t, 0, x, slot] = field[t, zb, c, x + 1, pl.ds(TOP, 1)]
                    edge_out[t, 1, x, slot] = field[t, zb, c, x + 1, pl.ds(TOP + ny - 1, 1)]

    def send_corners(t, side):
        for dy in (0, 1):
            @pl.when(has_x[side] & has_y[dy])
            def _():
                corner(t, side, dy).start()

    def send_edges(t, group):
        for dy in (0, 1):
            @pl.when(has_y[dy])
            def _():
                edge(t, dy, group).start()

    def receive_edges(t, group):
        planes = (rim[CROSS],) if group == CROSS else tuple(early + i for i in range(nx - 1))
        for dy in (0, 1):
            @pl.when(has_y[1 - dy])
            def _():
                edge(t, dy, group).wait_recv()
                row = (TOP + ny, TOP - 1)[dy]
                for x in planes:
                    for zb in range(nzb):
                        for c in (0, 1):
                            field[t, zb, c, x + 1, pl.ds(row, 1)] = edge_in[t, dy, x, pl.ds(zb * 2 + c, 1)]

    def receive_face(t, side):
        for dy in (0, 1):
            @pl.when(has_x[side] & has_y[1 - dy])
            def _():
                corner(t, side, dy).wait_recv()
                row = (TOP + ny, TOP - 1)[dy]
                for zb in range(nzb):
                    for c in (0, 1):
                        field[t, zb, c, halo[side], pl.ds(row, 1)] = corner_in[
                            t, side, dy, pl.ds(zb * 2 + c, 1)
                        ]
        @pl.when(has_x[side])
        def _():
            face(t, side).wait_recv()

    arrived("now")
    stage_edges(0, range(nx))
    pl.semaphore_wait(barrier, greeted)
    send_corners(0, CROSS)
    for side in (CROSS, CHIP):
        @pl.when(has_x[side])
        def _():
            for zb in range(nzb):
                first_face(zb, side).start()
    for group in (CHIP, CROSS):
        send_edges(0, group)
    send_corners(0, CHIP)

    arrived("angle")
    arrived("params")

    @pl.loop(0, nx)
    def _(x):
        for tile in range(tiles):
            rows = pl.ds(tile * ROWS, ROWS)
            for zb in range(nzb):
                cols = lanes_of(zb)
                tilt = levels[0, x, rows, cols].astype(F32)
                turn = levels[1, x, rows, cols].astype(F32)
                sin_h, cos_h = sin_cos_small(tilt * (0.5 * math.pi / LEVELS) - 0.25 * math.pi)
                sin_t = (sin_h + cos_h) * math.sqrt(0.5)
                cos_t = (cos_h - sin_h) * math.sqrt(0.5)
                sin_q, cos_q = sin_cos_small(turn * (0.5 * math.pi / LEVELS) - 0.25 * math.pi)
                sin_2, cos_2 = 2.0 * sin_q * cos_q, 1.0 - 2.0 * sin_q * sin_q
                sin_p, cos_p = -2.0 * sin_2 * cos_2, 2.0 * sin_2 * sin_2 - 1.0
                flat = sin_t * sin_t
                slope = 0.5 * sin_t * cos_t
                coef[0, x, zb, rows] = flat * cos_p * cos_p
                coef[1, x, zb, rows] = flat * sin_p * sin_p
                coef[2, x, zb, rows] = cos_t * cos_t
                coef[3, x, zb, rows] = 0.5 * flat * sin_p * cos_p
                coef[4, x, zb, rows] = slope * sin_p
                coef[5, x, zb, rows] = slope * cos_p
                vel = params[0, x, rows, cols]
                coef[6, x, zb, rows] = vel * vel
                coef[7, x, zb, rows] = 1.0 + 2.0 * params[1, x, rows, cols]
                coef[8, x, zb, rows] = jnp.sqrt(1.0 + 2.0 * params[2, x, rows, cols])

    arrived("channels")
    cell = cells[...]
    local_x = cell // width_y - gx * nx
    local_y = cell % width_y - gy * ny
    slots = lax.broadcasted_iota(jnp.int32, cell.shape, 1)
    inside = (local_x >= 0) & (local_x < nx) & (local_y >= 0) & (local_y < ny) & (slots < count_ref[0])
    target = jnp.where(inside, local_x * ny + local_y, -1)
    spots = lax.broadcasted_iota(jnp.int32, (nx * ny, cell.shape[1]), 0)
    onehot = jnp.where(target == spots, 1.0, 0.0).astype(BF16)
    value = traces[...]
    high = value.astype(BF16).astype(F32)
    middle = (value - high).astype(BF16).astype(F32)
    low = (value - high) - middle
    parts[...] = jnp.zeros_like(parts)
    parts[pl.ds(0, steps)] = high
    parts[pl.ds(steps, steps)] = middle
    parts[pl.ds(2 * steps, steps)] = low
    table = lax.dot_general(
        onehot, parts[...].astype(BF16), (((1,), (1,)), ((), ())), preferred_element_type=F32
    )
    table = table + pltpu.roll(table, LANES - steps, 1) + pltpu.roll(table, LANES - 2 * steps, 1)
    spot_lane = lax.broadcasted_iota(jnp.int32, table.shape, 1)
    for t in range(steps):
        moved = table if t == 0 else pltpu.roll(table, LANES - t, 1)
        surf[t] = jnp.where(spot_lane == 0, moved, 0.0)

    lane = lax.broadcasted_iota(jnp.int32, (ROWS, LANES), 1)
    first, last = lane == 0, lane == LANES - 1
    zero = jnp.zeros((ROWS, LANES), F32)

    def shifted(blocks):
        ahead = [pltpu.roll(block, LANES - 1, 1) for block in blocks] + [zero]
        behind = [zero] + [pltpu.roll(block, 1, 1) for block in blocks]
        after = [jnp.where(last, ahead[i + 1], ahead[i]) for i in range(nzb)]
        prior = [jnp.where(first, behind[i], behind[i + 1]) for i in range(nzb)]
        return after, prior

    def stencil(t, c, x, tile, weights):
        def read(dx, dy):
            rows = pl.ds(TOP + tile * ROWS + dy, ROWS)
            return [field[t, zb, c, x + 1 + dx, rows] for zb in range(nzb)]

        center, right, left, north, south = read(0, 0), read(1, 0), read(-1, 0), read(0, 1), read(0, -1)
        slope_y = [a - b for a, b in zip(north, south)]
        slope_x = [a - b for a, b in zip(right, left)]
        cross = [(a - b) - (d - e) for a, b, d, e in zip(read(1, 1), read(1, -1), read(-1, 1), read(-1, -1))]
        after, prior = shifted(center)
        after_y, prior_y = shifted(slope_y)
        after_x, prior_x = shifted(slope_x)
        out = []
        for zb in range(nzb):
            w = weights[zb]
            sum_x = right[zb] + left[zb]
            sum_y = north[zb] + south[zb]
            sum_z = after[zb] + prior[zb]
            mixed = (
                w[0] * sum_x
                + w[1] * sum_y
                + w[2] * sum_z
                + w[3] * cross[zb]
                + w[4] * (after_y[zb] - prior_y[zb])
                + w[5] * (after_x[zb] - prior_x[zb])
            )
            twice = center[zb] + center[zb]
            if c == 0:
                out.append((sum_x + sum_y + sum_z) - (twice + twice) - mixed)
            else:
                out.append(mixed - twice)
        return out

    def advance(t, x, tile):
        rows = pl.ds(tile * ROWS, ROWS)
        for zb in range(nzb):
            cols = lanes_of(zb)
            horiz, axial = ha[0, x, zb, rows], ha[1, x, zb, rows]
            speed, stretch, root = (coef[i, x, zb, rows] for i in (6, 7, 8))
            updates = (stretch * horiz + root * axial, root * horiz + axial)
            for c in (0, 1):
                here = pl.ds(TOP + tile * ROWS, ROWS)
                center = field[t, zb, c, x + 1, here]
                old = before[c, x, rows, cols] if t == 0 else field[t - 1, zb, c, x + 1, here]
                following = (center + center) - old + speed * updates[c]
                if zb == 0 and c == 0:
                    start = pl.multiple_of(x * ny + tile * ROWS, ROWS)
                    following = following + surf[t, pl.ds(start, ROWS)]
                if t == steps - 1:
                    result[c, x, rows, cols] = following
                else:
                    field[t + 1, zb, c, x + 1, here] = following

    def operators(t, x):
        for tile in range(tiles):
            rows = pl.ds(tile * ROWS, ROWS)
            weights = [[coef[i, x, zb, rows] for i in range(6)] for zb in range(nzb)]
            for c in (0, 1):
                out = stencil(t, c, x, tile, weights)
                for zb in range(nzb):
                    ha[c, x, zb, rows] = out[zb]
            advance(t, x, tile)

    parts_of = (tuple(range(1, tiles - 1)), (0, tiles - 1))
    depth_of = ny // 2

    def place(tile):
        return pl.ds((parts_of[0] + parts_of[1]).index(tile) * ROWS, ROWS)

    def widen(x):
        for zb in range(nzb):
            for c in (0, 1):
                wide[c, x, zb] = forward[steps - 1, c, x, :, lanes_of(zb)].astype(F32)

    def finish(x, part):
        t = steps - 1
        for tile in parts_of[part]:
            rows = pl.ds(tile * ROWS, ROWS)
            weights = [[coef[i, x, zb, rows] for i in range(6)] for zb in range(nzb)]
            horiz, axial = (stencil(t, c, x, tile, weights) for c in (0, 1))
            for zb in range(nzb):
                ha[0, x, zb, rows] = horiz[zb]
                ha[1, x, zb, rows] = axial[zb]
                pf, qf = wide[0, x, zb, rows], wide[1, x, zb, rows]
                terms = (pf * horiz[zb], pf * axial[zb] + qf * horiz[zb], qf * axial[zb])
                for i in range(3):
                    sums[zb, i, x, place(tile)] = sums[zb, i, x, place(tile)] + terms[i]
        far(x, part).start()
        single(x, part).start()

    def accumulate(t, x):
        for half in range(ny // 16):
            rows = pl.ds(half * 16, 16)
            for zb in range(nzb):
                cols = lanes_of(zb)
                horiz, axial = ha[0, x, zb, rows], ha[1, x, zb, rows]
                pf = forward[t, 0, x, rows, cols].astype(F32)
                qf = forward[t, 1, x, rows, cols].astype(F32)
                terms = (pf * horiz, pf * axial + qf * horiz, qf * axial)
                for i in range(3):
                    for j in (0, 1):
                        spot = place(2 * half + j)
                        term = terms[i][j * ROWS : (j + 1) * ROWS]
                        sums[zb, i, x, spot] = term if t == 0 else sums[zb, i, x, spot] + term

    half = nx // 2

    def onward(x):
        return jnp.where(x < half, up, down)

    def back(x):
        return jnp.where(x < half, down, up)

    def rows_of(part):
        return pl.ds(part * depth_of, depth_of)

    def far(x, part):
        return pltpu.make_async_remote_copy(
            src_ref=sums.at[across, :, x, rows_of(part)],
            dst_ref=far_in.at[part, x],
            send_sem=fs.at[part, x],
            recv_sem=fr.at[part, x],
            device_id={"src": onward(x)},
            device_id_type=MESH,
        )

    def near(x, part, peer, slot):
        return pltpu.make_async_remote_copy(
            src_ref=sums.at[peer, :, x, rows_of(part)],
            dst_ref=near_in.at[slot, part, x],
            send_sem=ns.at[slot, part, x],
            recv_sem=nr.at[slot, part, x],
            device_id={"src": peer},
            device_id_type=MESH,
        )

    def joined(x, part):
        return near(x, part, onward(x), 0)

    def single(x, part):
        return near(x, part, back(x), 1)

    order = [rim[CHIP] - sign * i for i in range(nx)]
    arrived("before")
    for t in range(steps - 1):
        receive_edges(t, CHIP)
        receive_face(t, CHIP)

        @pl.loop(0, nx - 2)
        def _(i):
            operators(t, rim[CHIP] - sign * i)

        receive_edges(t, CROSS)
        operators(t, order[nx - 2])
        stage_edges(t + 1, order[: nx - 1])
        send_face(t + 1, CHIP)
        send_edges(t + 1, CHIP)
        send_corners(t + 1, CHIP)
        if t == 0:
            arrived("forward")

        @pl.loop(0, nx - 1)
        def _(i):
            accumulate(t, rim[CHIP] - sign * i)

        if t == steps - 2:
            finish(order[1], 0)
        receive_face(t, CROSS)
        operators(t, order[nx - 1])
        stage_edges(t + 1, order[nx - 1 :])
        send_corners(t + 1, CROSS)
        send_face(t + 1, CROSS)
        send_edges(t + 1, CROSS)
        accumulate(t, order[nx - 1])
        if t == 0:
            @pl.loop(0, nx)
            def _(x):
                widen(x)

    final = steps - 1
    finish(order[2], 0)
    receive_face(final, CHIP)
    finish(order[0], 0)
    receive_edges(final, CHIP)
    finish(order[0], 1)
    finish(order[1], 1)
    receive_edges(final, CROSS)
    finish(order[2], 1)
    receive_face(final, CROSS)
    finish(order[3], 0)
    finish(order[3], 1)
    sequence = [(1, 0), (2, 0), (0, 0), (0, 1), (1, 1), (2, 1), (3, 0), (3, 1)]
    sequence = [(order[i], part) for i, part in sequence]

    @pl.loop(0, nx)
    def _(x):
        for tile in range(tiles):
            advance(steps - 1, x, tile)

    out_copy = pltpu.make_async_copy(result, next_hbm.at[0], out_sem.at[0])
    out_copy.start()
    for x, part in sequence:
        far(x, part).wait_recv()
        for i in range(3):
            here = sums.at[onward(x), i, x, rows_of(part)]
            here[...] = here[...] + far_in[part, x, i]
        joined(x, part).start()

    arrived("own")
    for x, part in sequence:
        single(x, part).wait_recv()
        joined(x, part).wait_recv()
        for j, tile in enumerate(parts_of[part]):
            rows = pl.ds(tile * ROWS, ROWS)
            spot = pl.ds(j * ROWS, ROWS)
            a, b, c = (
                sums[me, i, x, place(tile)] + near_in[0, part, x, i, spot] + near_in[1, part, x, i, spot]
                for i in range(3)
            )
            vel = own[0, x, rows]
            stretch = 1.0 + 2.0 * own[1, x, rows]
            root = jnp.sqrt(1.0 + 2.0 * own[2, x, rows])
            speed = vel * vel
            grads[0, x, rows] = 2.0 * vel * (stretch * a + root * b + c)
            grads[1, x, rows] = 2.0 * speed * a
            grads[2, x, rows] = speed / root * b
    grad_copies = [
        pltpu.make_async_copy(grads.at[i], out, out_sem.at[1 + i])
        for i, out in enumerate((gvel_hbm, geps_hbm, gdelta_hbm))
    ]
    for copy in grad_copies:
        copy.start()

    for t in range(steps):
        for side in (CROSS, CHIP):
            @pl.when(has_x[side])
            def _():
                face(t, side).wait_send()
        for dy in (0, 1):
            @pl.when(has_y[dy])
            def _():
                for group in (CROSS, CHIP):
                    edge(t, dy, group).wait_send()
            for side in (CROSS, CHIP):
                @pl.when(has_x[side] & has_y[dy])
                def _():
                    corner(t, side, dy).wait_send()
    for x, part in sequence:
        far(x, part).wait_send()
        joined(x, part).wait_send()
        single(x, part).wait_send()
    out_copy.wait()
    for copy in grad_copies:
        copy.wait()


def copy_kernel(*refs):
    sources, targets, stages = refs[:4], refs[4:8], refs[8:12]
    fetched, stored = refs[12:]
    pieces = [(0, (0, c, x)) for c in (0, 1) for x in range(sources[0].shape[2])]
    pieces += [(i, ()) for i in (1, 2, 3)]
    fetches, stores = [], []
    for slot, (i, at) in enumerate(pieces):
        source, stage, target = (ref.at[at] if at else ref for ref in (sources[i], stages[i], targets[i]))
        fetches.append(pltpu.make_async_copy(source, stage, fetched.at[slot]))
        stores.append(pltpu.make_async_copy(stage, target, stored.at[slot]))
    for fetch in fetches:
        fetch.start()
    for fetch, store in zip(fetches, stores):
        fetch.wait()
        store.start()
    for store in stores:
        store.wait()


def hand_out(results):
    anywhere = pl.BlockSpec(memory_space=pl.ANY)
    pieces = 2 * results[0].shape[2] + 3
    return pl.pallas_call(
        copy_kernel,
        name="hand_out",
        out_shape=tuple(jax.ShapeDtypeStruct(r.shape, r.dtype) for r in results),
        in_specs=[anywhere] * len(results),
        out_specs=(anywhere,) * len(results),
        scratch_shapes=[pltpu.VMEM(r.shape, r.dtype) for r in results] + [pltpu.SemaphoreType.DMA((pieces,))] * 2,
        compiler_params=pltpu.CompilerParams(vmem_limit_bytes=60 * 1024 * 1024),
    )(*results)


def on_device(
    adjoint_now,
    adjoint_before,
    forward_field,
    velocity,
    thomsen_eps,
    thomsen_delta,
    tilt_level,
    azimuth_level,
    channel_cell,
    channel_count,
    residual_trace,
):
    nx, ny, depth = velocity.shape
    nzb = depth // LANES
    steps = forward_field.shape[0]
    channels = channel_cell.shape[1]
    size_x, size_y, size_s = (lax.axis_size(name) for name in ("gx", "gy", "src"))
    block = jax.ShapeDtypeStruct((nx, ny, LANES), F32)
    anywhere = pl.BlockSpec(memory_space=pl.ANY)
    dma = pltpu.SemaphoreType.DMA
    results = pl.pallas_call(
        functools.partial(kernel, size_x, size_y, size_s, ny * size_y),
        name="adjoint_steps",
        out_shape=(jax.ShapeDtypeStruct(adjoint_now.shape, F32), block, block, block),
        in_specs=[anywhere] * 9 + [pl.BlockSpec(memory_space=pltpu.SMEM), anywhere],
        out_specs=(anywhere,) * 4,
        scratch_shapes=[
            pltpu.VMEM((steps, nzb, 2, nx + 2, ny + 2 * TOP, LANES), F32),
            pltpu.VMEM((2, nx, ny, depth), F32),
            pltpu.VMEM((steps, 2, nx, ny, depth), BF16),
            pltpu.VMEM((2, nx, nzb, ny, LANES), F32),
            pltpu.VMEM((3, nx, ny, depth), F32),
            pltpu.VMEM((2, nx, ny, depth), jnp.int32),
            pltpu.VMEM((3, nx, ny, LANES), F32),
            pltpu.VMEM((1, channels), jnp.int32),
            pltpu.VMEM((steps, channels), F32),
            pltpu.VMEM((LANES, channels), F32),
            pltpu.VMEM((9, nx, nzb, ny, LANES), F32),
            pltpu.VMEM((steps, nx * ny, LANES), F32),
            pltpu.VMEM((2, nx, nzb, ny, LANES), F32),
            pltpu.VMEM((nzb, 3, nx, ny, LANES), F32),
            pltpu.VMEM((steps, 2, nx, 2 * nzb, LANES), F32),
            pltpu.VMEM((steps, 2, nx, 2 * nzb, LANES), F32),
            pltpu.VMEM((steps, 2, 2, 2 * nzb, LANES), F32),
            pltpu.VMEM((2, nx, 3, ny // 2, LANES), F32),
            pltpu.VMEM((2, 2, nx, 3, ny // 2, LANES), F32),
            pltpu.VMEM((2, nx, ny, depth), F32),
            pltpu.VMEM((3, nx, ny, LANES), F32),
            dma((nzb + 12,)),
            dma((4,)),
            dma((steps, 2)),
            dma((steps, 2)),
            dma((steps, 2, 2)),
            dma((steps, 2, 2)),
            dma((steps, 2, 2)),
            dma((steps, 2, 2)),
            dma((2, nx)),
            dma((2, nx)),
            dma((2, 2, nx)),
            dma((2, 2, nx)),
        ],
        compiler_params=pltpu.CompilerParams(
            collective_id=0, has_side_effects=True, vmem_limit_bytes=60 * 1024 * 1024
        ),
    )(
        adjoint_now,
        adjoint_before,
        forward_field,
        velocity,
        thomsen_eps,
        thomsen_delta,
        tilt_level,
        azimuth_level,
        channel_cell,
        channel_count,
        jnp.transpose(residual_trace, (1, 0, 2)),
    )
    return hand_out(results)


def solution(mesh):
    placed = (
        P("src", None, "gx", "gy", None),
        P("src", None, "gx", "gy", None),
        P(None, "src", None, "gx", "gy", None),
        P("gx", "gy", None),
        P("gx", "gy", None),
        P("gx", "gy", None),
        P("gx", "gy", None),
        P("gx", "gy", None),
        P("src", None),
        P("src"),
        P("src", None, None),
    )
    return jax.shard_map(
        on_device,
        mesh=mesh,
        in_specs=placed,
        out_specs=(
            P("src", None, "gx", "gy", None),
            P("gx", "gy", "src"),
            P("gx", "gy", "src"),
            P("gx", "gy", "src"),
        ),
        check_vma=False,
    )
```

```python
import functools
import math

import jax
import jax.numpy as jnp
from jax import lax
from jax.experimental import pallas as pl
from jax.experimental.pallas import tpu as pltpu
from jax.sharding import PartitionSpec as P

LEVELS = 32
LANES = 128
ROWS = 8
TOP = 8
MESH = pl.DeviceIdType.MESH
CROSS, CHIP = 0, 1
F32 = jnp.float32
BF16 = jnp.bfloat16


def sin_cos_small(angle):
    sq = angle * angle
    sin = angle + angle * sq * (-1.0 / 6 + sq * (1.0 / 120 + sq * (-1.0 / 5040 + sq * (1.0 / 362880))))
    cos = 1.0 + sq * (-0.5 + sq * (1.0 / 24 + sq * (-1.0 / 720 + sq * (1.0 / 40320 - sq * (1.0 / 3628800)))))
    return sin, cos


def kernel(
    size_x,
    size_y,
    size_s,
    width_y,
    now_hbm,
    before_hbm,
    forward_hbm,
    vel_hbm,
    eps_hbm,
    delta_hbm,
    tilt_hbm,
    azimuth_hbm,
    cell_hbm,
    count_ref,
    trace_hbm,
    next_hbm,
    gvel_hbm,
    geps_hbm,
    gdelta_hbm,
    field,
    before,
    forward,
    wide,
    params,
    levels,
    own,
    cells,
    traces,
    parts,
    coef,
    surf,
    ha,
    sums,
    edge_out,
    edge_in,
    corner_in,
    far_in,
    near_in,
    result,
    grads,
    load_sem,
    out_sem,
    xs,
    xr,
    ys,
    yr,
    cs,
    cr,
    fs,
    fr,
    ns,
    nr,
):
    gx, gy, me = lax.axis_index("gx"), lax.axis_index("gy"), lax.axis_index("src")
    steps = 3
    nx = now_hbm.shape[2]
    ny = now_hbm.shape[3]
    nzb = now_hbm.shape[4] // LANES
    tiles = ny // ROWS
    body = pl.ds(TOP, ny)
    even = lax.rem(gx, 2) == 0
    below, above = gx > 0, gx < size_x - 1
    has_x = (even & below | ~even & above, even & above | ~even & below)
    sign = jnp.where(even, 1, -1)
    to_x = (gx - sign, gx + sign)
    rim = (jnp.where(even, 0, nx - 1), jnp.where(even, nx - 1, 0))
    halo = (jnp.where(even, 0, nx + 1), jnp.where(even, nx + 1, 0))
    landing = (halo[1], halo[0])
    early = jnp.where(even, 1, 0)
    has_y = (gy > 0, gy < size_y - 1)
    to_y = (gy - 1, gy + 1)
    up = lax.rem(me + 1, size_s)
    down = lax.rem(me + size_s - 1, size_s)
    across = lax.rem(me + 2, size_s)

    def lanes_of(zb):
        return pl.ds(zb * LANES, LANES)

    loads = {}

    def load(name, index, src, dst):
        loads.setdefault(name, []).append(pltpu.make_async_copy(src, dst, load_sem.at[index]))

    for zb in range(nzb):
        load("now", zb, now_hbm.at[0, :, :, :, lanes_of(zb)], field.at[0, zb, :, pl.ds(1, nx), body, :])
    load("angle", nzb, tilt_hbm, levels.at[0])
    load("angle", nzb + 1, azimuth_hbm, levels.at[1])
    load("params", nzb + 2, vel_hbm, params.at[0])
    load("params", nzb + 3, eps_hbm, params.at[1])
    load("params", nzb + 4, delta_hbm, params.at[2])
    load("channels", nzb + 5, cell_hbm, cells)
    load("channels", nzb + 6, trace_hbm.at[:, 0], traces)
    load("before", nzb + 7, before_hbm.at[0], before)
    load("forward", nzb + 8, forward_hbm.at[:, 0], forward)
    mine = pl.ds(pl.multiple_of(me * LANES, LANES), LANES)
    load("own", nzb + 9, vel_hbm.at[:, :, mine], own.at[0])
    load("own", nzb + 10, eps_hbm.at[:, :, mine], own.at[1])
    load("own", nzb + 11, delta_hbm.at[:, :, mine], own.at[2])
    def arrived(name):
        for copy in loads[name]:
            copy.wait()

    barrier = pltpu.get_barrier_semaphore()
    greeted = jnp.int32(2)
    for side in (CROSS, CHIP):
        for dy in (0, 1):
            both = has_x[side] & has_y[dy]
            @pl.when(both)
            def _():
                pl.semaphore_signal(
                    barrier, inc=1, device_id={"gx": to_x[side], "gy": to_y[dy]}, device_id_type=MESH
                )
            greeted = greeted + both.astype(jnp.int32)
    for peer in (up, down):
        pl.semaphore_signal(barrier, inc=1, device_id={"src": peer}, device_id_type=MESH)
    for side in (CROSS, CHIP):
        @pl.when(has_x[side])
        def _():
            pl.semaphore_signal(barrier, inc=1, device_id={"gx": to_x[side]}, device_id_type=MESH)
        greeted = greeted + has_x[side].astype(jnp.int32)
    for dy in (0, 1):
        @pl.when(has_y[dy])
        def _():
            pl.semaphore_signal(barrier, inc=1, device_id={"gy": to_y[dy]}, device_id_type=MESH)
        greeted = greeted + has_y[dy].astype(jnp.int32)

    for group in loads.values():
        for copy in group:
            copy.start()

    for side in (CROSS, CHIP):
        @pl.when(jnp.logical_not(has_x[side]))
        def _():
            zeros = jnp.zeros((ny + 2 * TOP, LANES), F32)
            @pl.loop(0, steps)
            def _(t):
                for zb in range(nzb):
                    for c in (0, 1):
                        field[t, zb, c, halo[side]] = zeros
    for dy in (0, 1):
        @pl.when(jnp.logical_not(has_y[dy]))
        def _():
            row = (TOP - 1, TOP + ny)[dy]
            zeros = jnp.zeros((1, LANES), F32)
            @pl.loop(0, steps)
            def _(t):
                for zb in range(nzb):
                    for c in (0, 1):
                        for x in range(nx + 2):
                            field[t, zb, c, x, pl.ds(row, 1)] = zeros

    def face(t, side):
        return pltpu.make_async_remote_copy(
            src_ref=field.at[t, :, :, rim[side] + 1, body, :],
            dst_ref=field.at[t, :, :, landing[side], body, :],
            send_sem=xs.at[t, side],
            recv_sem=xr.at[t, side],
            device_id={"gx": to_x[side]},
            device_id_type=MESH,
        )

    def first_face(zb, side):
        return pltpu.make_async_remote_copy(
            src_ref=now_hbm.at[0, :, rim[side], :, lanes_of(zb)],
            dst_ref=field.at[0, zb, :, landing[side], body, :],
            send_sem=xs.at[0, side],
            recv_sem=xr.at[0, side],
            device_id={"gx": to_x[side]},
            device_id_type=MESH,
        )

    def planes_of(group):
        return pl.ds(rim[CROSS], 1) if group == CROSS else pl.ds(early, nx - 1)

    def edge(t, dy, group):
        return pltpu.make_async_remote_copy(
            src_ref=edge_out.at[t, dy, planes_of(group)],
            dst_ref=edge_in.at[t, dy, planes_of(group)],
            send_sem=ys.at[t, dy, group],
            recv_sem=yr.at[t, dy, group],
            device_id={"gy": to_y[dy]},
            device_id_type=MESH,
        )

    def corner(t, side, dy):
        return pltpu.make_async_remote_copy(
            src_ref=edge_out.at[t, dy, rim[side]],
            dst_ref=corner_in.at[t, side, dy],
            send_sem=cs.at[t, side, dy],
            recv_sem=cr.at[t, side, dy],
            device_id={"gx": to_x[side], "gy": to_y[dy]},
            device_id_type=MESH,
        )

    def send_face(t, side):
        @pl.when(has_x[side])
        def _():
            face(t, side).start()

    def stage_edges(t, planes):
        for x in planes:
            for zb in range(nzb):
                for c in (0, 1):
                    slot = pl.ds(zb * 2 + c, 1)
                    edge_out[t, 0, x, slot] = field[t, zb, c, x + 1, pl.ds(TOP, 1)]
                    edge_out[t, 1, x, slot] = field[t, zb, c, x + 1, pl.ds(TOP + ny - 1, 1)]

    def send_corners(t, side):
        for dy in (0, 1):
            @pl.when(has_x[side] & has_y[dy])
            def _():
                corner(t, side, dy).start()

    def send_edges(t, group):
        for dy in (0, 1):
            @pl.when(has_y[dy])
            def _():
                edge(t, dy, group).start()

    def receive_edges(t, group):
        planes = (rim[CROSS],) if group == CROSS else tuple(early + i for i in range(nx - 1))
        for dy in (0, 1):
            @pl.when(has_y[1 - dy])
            def _():
                edge(t, dy, group).wait_recv()
                row = (TOP + ny, TOP - 1)[dy]
                for x in planes:
                    for zb in range(nzb):
                        for c in (0, 1):
                            field[t, zb, c, x + 1, pl.ds(row, 1)] = edge_in[t, dy, x, pl.ds(zb * 2 + c, 1)]

    def receive_face(t, side):
        for dy in (0, 1):
            @pl.when(has_x[side] & has_y[1 - dy])
            def _():
                corner(t, side, dy).wait_recv()
                row = (TOP + ny, TOP - 1)[dy]
                for zb in range(nzb):
                    for c in (0, 1):
                        field[t, zb, c, halo[side], pl.ds(row, 1)] = corner_in[
                            t, side, dy, pl.ds(zb * 2 + c, 1)
                        ]
        @pl.when(has_x[side])
        def _():
            face(t, side).wait_recv()

    arrived("now")
    stage_edges(0, range(nx))
    pl.semaphore_wait(barrier, greeted)
    send_corners(0, CROSS)
    for side in (CROSS, CHIP):
        @pl.when(has_x[side])
        def _():
            for zb in range(nzb):
                first_face(zb, side).start()
    for group in (CHIP, CROSS):
        send_edges(0, group)
    send_corners(0, CHIP)

    lane = lax.broadcasted_iota(jnp.int32, (ROWS, LANES), 1)
    first, last = lane == 0, lane == LANES - 1
    zero = jnp.zeros((ROWS, LANES), F32)

    def shifted(blocks):
        ahead = [pltpu.roll(block, LANES - 1, 1) for block in blocks] + [zero]
        behind = [zero] + [pltpu.roll(block, 1, 1) for block in blocks]
        after = [jnp.where(last, ahead[i + 1], ahead[i]) for i in range(nzb)]
        prior = [jnp.where(first, behind[i], behind[i + 1]) for i in range(nzb)]
        return after, prior

    arrived("angle")
    arrived("params")

    @pl.loop(0, nx)
    def _(x):
        for tile in range(tiles):
            rows = pl.ds(tile * ROWS, ROWS)
            deep = ([], [], [])
            for zb in range(nzb):
                cols = lanes_of(zb)
                tilt = levels[0, x, rows, cols].astype(F32)
                turn = levels[1, x, rows, cols].astype(F32)
                sin_h, cos_h = sin_cos_small(tilt * (0.5 * math.pi / LEVELS) - 0.25 * math.pi)
                sin_t = (sin_h + cos_h) * math.sqrt(0.5)
                cos_t = (cos_h - sin_h) * math.sqrt(0.5)
                sin_q, cos_q = sin_cos_small(turn * (0.5 * math.pi / LEVELS) - 0.25 * math.pi)
                sin_2, cos_2 = 2.0 * sin_q * cos_q, 1.0 - 2.0 * sin_q * sin_q
                sin_p, cos_p = -2.0 * sin_2 * cos_2, 2.0 * sin_2 * sin_2 - 1.0
                flat = sin_t * sin_t
                slope = 0.5 * sin_t * cos_t
                coef[0, x, zb, rows] = flat * cos_p * cos_p
                coef[1, x, zb, rows] = flat * sin_p * sin_p
                coef[3, x, zb, rows] = 0.5 * flat * sin_p * cos_p
                for weight, value in zip(deep, (cos_t * cos_t, slope * sin_p, slope * cos_p)):
                    weight.append(value)
                vel = params[0, x, rows, cols]
                coef[6, x, zb, rows] = vel * vel
                coef[7, x, zb, rows] = 1.0 + 2.0 * params[1, x, rows, cols]
                coef[8, x, zb, rows] = jnp.sqrt(1.0 + 2.0 * params[2, x, rows, cols])
            for slot, weight in zip((2, 4, 5), deep):
                after, prior = shifted(weight)
                for zb in range(nzb):
                    coef[slot, x, zb, rows] = prior[zb]
                    coef[{2: 9, 4: 10, 5: 11}[slot], x, zb, rows] = after[zb]

    arrived("channels")
    cell = cells[...]
    local_x = cell // width_y - gx * nx
    local_y = cell % width_y - gy * ny
    slots = lax.broadcasted_iota(jnp.int32, cell.shape, 1)
    inside = (local_x >= 0) & (local_x < nx) & (local_y >= 0) & (local_y < ny) & (slots < count_ref[0])
    target = jnp.where(inside, local_x * ny + local_y, -1)
    spots = lax.broadcasted_iota(jnp.int32, (nx * ny, cell.shape[1]), 0)
    onehot = jnp.where(target == spots, 1.0, 0.0).astype(BF16)
    value = traces[...]
    high = value.astype(BF16).astype(F32)
    middle = (value - high).astype(BF16).astype(F32)
    low = (value - high) - middle
    parts[...] = jnp.zeros_like(parts)
    parts[pl.ds(0, steps)] = high
    parts[pl.ds(steps, steps)] = middle
    parts[pl.ds(2 * steps, steps)] = low
    table = lax.dot_general(
        onehot, parts[...].astype(BF16), (((1,), (1,)), ((), ())), preferred_element_type=F32
    )
    table = table + pltpu.roll(table, LANES - steps, 1) + pltpu.roll(table, LANES - 2 * steps, 1)
    spot_lane = lax.broadcasted_iota(jnp.int32, table.shape, 1)
    for t in range(steps):
        moved = table if t == 0 else pltpu.roll(table, LANES - t, 1)
        surf[t] = jnp.where(spot_lane == 0, moved, 0.0)

    def stencil(t, c, x, tile, weights):
        def read(dx, dy):
            rows = pl.ds(TOP + tile * ROWS + dy, ROWS)
            return [field[t, zb, c, x + 1 + dx, rows] for zb in range(nzb)]

        center, right, left, north, south = read(0, 0), read(1, 0), read(-1, 0), read(0, 1), read(0, -1)
        slope_y = [a - b for a, b in zip(north, south)]
        slope_x = [a - b for a, b in zip(right, left)]
        cross = [(a - b) - (d - e) for a, b, d, e in zip(read(1, 1), read(1, -1), read(-1, 1), read(-1, -1))]
        onto_prior, onto_after = [], []
        for zb in range(nzb):
            w, v = weights[zb], center[zb]
            ahead = w[2] * v + w[4] * slope_y[zb] + w[5] * slope_x[zb]
            behind = w[6] * v - w[7] * slope_y[zb] - w[8] * slope_x[zb]
            onto_prior.append(v - ahead if c == 0 else ahead)
            onto_after.append(v - behind if c == 0 else behind)
        after, _ = shifted(onto_prior)
        _, prior = shifted(onto_after)
        out = []
        for zb in range(nzb):
            w = weights[zb]
            sum_x = right[zb] + left[zb]
            sum_y = north[zb] + south[zb]
            mixed = w[0] * sum_x + w[1] * sum_y + w[3] * cross[zb]
            deep = after[zb] + prior[zb]
            twice = center[zb] + center[zb]
            if c == 0:
                out.append((sum_x + sum_y) - (twice + twice) - mixed + deep)
            else:
                out.append(mixed - twice + deep)
        return out

    def advance(t, x, tile):
        rows = pl.ds(tile * ROWS, ROWS)
        for zb in range(nzb):
            cols = lanes_of(zb)
            horiz, axial = ha[0, x, zb, rows], ha[1, x, zb, rows]
            speed, stretch, root = (coef[i, x, zb, rows] for i in (6, 7, 8))
            updates = (stretch * horiz + root * axial, root * horiz + axial)
            for c in (0, 1):
                here = pl.ds(TOP + tile * ROWS, ROWS)
                center = field[t, zb, c, x + 1, here]
                old = before[c, x, rows, cols] if t == 0 else field[t - 1, zb, c, x + 1, here]
                following = (center + center) - old + speed * updates[c]
                if zb == 0 and c == 0:
                    start = pl.multiple_of(x * ny + tile * ROWS, ROWS)
                    following = following + surf[t, pl.ds(start, ROWS)]
                if t == steps - 1:
                    result[c, x, rows, cols] = following
                else:
                    field[t + 1, zb, c, x + 1, here] = following

    def operators(t, x):
        for tile in range(tiles):
            rows = pl.ds(tile * ROWS, ROWS)
            weights = [[coef[i, x, zb, rows] for i in (0, 1, 2, 3, 4, 5, 9, 10, 11)] for zb in range(nzb)]
            for c in (0, 1):
                out = stencil(t, c, x, tile, weights)
                for zb in range(nzb):
                    ha[c, x, zb, rows] = out[zb]
            advance(t, x, tile)

    parts_of = (tuple(range(1, tiles - 1)), (0, tiles - 1))

    def place(tile):
        part = 0 if tile in parts_of[0] else 1
        return part, pl.ds(parts_of[part].index(tile) * ROWS, ROWS)

    def widen(x):
        for zb in range(nzb):
            for c in (0, 1):
                wide[c, x, zb] = forward[steps - 1, c, x, :, lanes_of(zb)].astype(F32)

    def finish(x, part):
        t = steps - 1
        for tile in parts_of[part]:
            rows = pl.ds(tile * ROWS, ROWS)
            weights = [[coef[i, x, zb, rows] for i in (0, 1, 2, 3, 4, 5, 9, 10, 11)] for zb in range(nzb)]
            horiz, axial = (stencil(t, c, x, tile, weights) for c in (0, 1))
            for zb in range(nzb):
                ha[0, x, zb, rows] = horiz[zb]
                ha[1, x, zb, rows] = axial[zb]
                pf, qf = wide[0, x, zb, rows], wide[1, x, zb, rows]
                terms = (pf * horiz[zb], pf * axial[zb] + qf * horiz[zb], qf * axial[zb])
                for i in range(3):
                    spot = place(tile)[1]
                    sums[zb, part, x, i, spot] = sums[zb, part, x, i, spot] + terms[i]
        far(x, part).start()
        single(x, part).start()

    def accumulate(t, x):
        for half in range(ny // 16):
            rows = pl.ds(half * 16, 16)
            for zb in range(nzb):
                cols = lanes_of(zb)
                horiz, axial = ha[0, x, zb, rows], ha[1, x, zb, rows]
                pf = forward[t, 0, x, rows, cols].astype(F32)
                qf = forward[t, 1, x, rows, cols].astype(F32)
                terms = (pf * horiz, pf * axial + qf * horiz, qf * axial)
                for i in range(3):
                    for j in (0, 1):
                        part, spot = place(2 * half + j)
                        term = terms[i][j * ROWS : (j + 1) * ROWS]
                        sums[zb, part, x, i, spot] = term if t == 0 else sums[zb, part, x, i, spot] + term

    half = nx // 2

    def onward(x):
        return jnp.where(x < half, up, down)

    def back(x):
        return jnp.where(x < half, down, up)

    def far(x, part):
        return pltpu.make_async_remote_copy(
            src_ref=sums.at[across, part, x],
            dst_ref=far_in.at[part, x],
            send_sem=fs.at[part, x],
            recv_sem=fr.at[part, x],
            device_id={"src": onward(x)},
            device_id_type=MESH,
        )

    def near(x, part, peer, slot):
        return pltpu.make_async_remote_copy(
            src_ref=sums.at[peer, part, x],
            dst_ref=near_in.at[slot, part, x],
            send_sem=ns.at[slot, part, x],
            recv_sem=nr.at[slot, part, x],
            device_id={"src": peer},
            device_id_type=MESH,
        )

    def joined(x, part):
        return near(x, part, onward(x), 0)

    def single(x, part):
        return near(x, part, back(x), 1)

    order = [rim[CHIP] - sign * i for i in range(nx)]
    arrived("before")
    for t in range(steps - 1):
        receive_edges(t, CHIP)
        receive_face(t, CHIP)

        @pl.loop(0, nx - 2)
        def _(i):
            operators(t, rim[CHIP] - sign * i)

        receive_edges(t, CROSS)
        operators(t, order[nx - 2])
        stage_edges(t + 1, order[: nx - 1])
        send_face(t + 1, CHIP)
        send_edges(t + 1, CHIP)
        send_corners(t + 1, CHIP)
        if t == 0:
            arrived("forward")

        @pl.loop(0, nx - 1)
        def _(i):
            accumulate(t, rim[CHIP] - sign * i)

        if t == steps - 2:
            finish(order[1], 0)
        receive_face(t, CROSS)
        operators(t, order[nx - 1])
        stage_edges(t + 1, order[nx - 1 :])
        send_corners(t + 1, CROSS)
        send_face(t + 1, CROSS)
        send_edges(t + 1, CROSS)
        accumulate(t, order[nx - 1])
        if t == 0:
            @pl.loop(0, nx)
            def _(x):
                widen(x)

    final = steps - 1
    finish(order[2], 0)
    receive_face(final, CHIP)
    finish(order[0], 0)
    receive_edges(final, CHIP)
    finish(order[0], 1)
    finish(order[1], 1)
    receive_edges(final, CROSS)
    finish(order[2], 1)
    receive_face(final, CROSS)
    finish(order[3], 0)
    finish(order[3], 1)
    sequence = [(1, 0), (2, 0), (0, 0), (0, 1), (1, 1), (2, 1), (3, 0), (3, 1)]
    sequence = [(order[i], part) for i, part in sequence]

    @pl.loop(0, nx)
    def _(x):
        for tile in range(tiles):
            advance(steps - 1, x, tile)

    out_copy = pltpu.make_async_copy(result, next_hbm.at[0], out_sem.at[0])
    out_copy.start()
    for x, part in sequence:
        far(x, part).wait_recv()
        here = sums.at[onward(x), part, x]
        here[...] = here[...] + far_in[part, x]
        joined(x, part).start()

    arrived("own")
    for x, part in sequence:
        single(x, part).wait_recv()
        joined(x, part).wait_recv()
        for j, tile in enumerate(parts_of[part]):
            rows = pl.ds(tile * ROWS, ROWS)
            spot = pl.ds(j * ROWS, ROWS)
            a, b, c = (
                sums[me, part, x, i, spot] + near_in[0, part, x, i, spot] + near_in[1, part, x, i, spot]
                for i in range(3)
            )
            vel = own[0, x, rows]
            stretch = 1.0 + 2.0 * own[1, x, rows]
            root = jnp.sqrt(1.0 + 2.0 * own[2, x, rows])
            speed = vel * vel
            grads[0, x, rows] = 2.0 * vel * (stretch * a + root * b + c)
            grads[1, x, rows] = 2.0 * speed * a
            grads[2, x, rows] = speed / root * b
    grad_copies = [
        pltpu.make_async_copy(grads.at[i], out, out_sem.at[1 + i])
        for i, out in enumerate((gvel_hbm, geps_hbm, gdelta_hbm))
    ]
    for copy in grad_copies:
        copy.start()

    for t in range(steps):
        for side in (CROSS, CHIP):
            @pl.when(has_x[side])
            def _():
                face(t, side).wait_send()
        for dy in (0, 1):
            @pl.when(has_y[dy])
            def _():
                for group in (CROSS, CHIP):
                    edge(t, dy, group).wait_send()
            for side in (CROSS, CHIP):
                @pl.when(has_x[side] & has_y[dy])
                def _():
                    corner(t, side, dy).wait_send()
    for x, part in sequence:
        far(x, part).wait_send()
        joined(x, part).wait_send()
        single(x, part).wait_send()
    out_copy.wait()
    for copy in grad_copies:
        copy.wait()


def copy_kernel(*refs):
    sources, targets, stages = refs[:4], refs[4:8], refs[8:12]
    fetched, stored = refs[12:]
    pieces = [(0, (0, c, x)) for c in (0, 1) for x in range(sources[0].shape[2])]
    pieces += [(i, ()) for i in (1, 2, 3)]
    fetches, stores = [], []
    for slot, (i, at) in enumerate(pieces):
        source, stage, target = (ref.at[at] if at else ref for ref in (sources[i], stages[i], targets[i]))
        fetches.append(pltpu.make_async_copy(source, stage, fetched.at[slot]))
        stores.append(pltpu.make_async_copy(stage, target, stored.at[slot]))
    for fetch in fetches:
        fetch.start()
    for fetch, store in zip(fetches, stores):
        fetch.wait()
        store.start()
    for store in stores:
        store.wait()


def hand_out(results):
    anywhere = pl.BlockSpec(memory_space=pl.ANY)
    pieces = 2 * results[0].shape[2] + 3
    return pl.pallas_call(
        copy_kernel,
        name="hand_out",
        out_shape=tuple(jax.ShapeDtypeStruct(r.shape, r.dtype) for r in results),
        in_specs=[anywhere] * len(results),
        out_specs=(anywhere,) * len(results),
        scratch_shapes=[pltpu.VMEM(r.shape, r.dtype) for r in results] + [pltpu.SemaphoreType.DMA((pieces,))] * 2,
        compiler_params=pltpu.CompilerParams(vmem_limit_bytes=60 * 1024 * 1024),
    )(*results)


def on_device(
    adjoint_now,
    adjoint_before,
    forward_field,
    velocity,
    thomsen_eps,
    thomsen_delta,
    tilt_level,
    azimuth_level,
    channel_cell,
    channel_count,
    residual_trace,
):
    nx, ny, depth = velocity.shape
    nzb = depth // LANES
    steps = forward_field.shape[0]
    channels = channel_cell.shape[1]
    size_x, size_y, size_s = (lax.axis_size(name) for name in ("gx", "gy", "src"))
    block = jax.ShapeDtypeStruct((nx, ny, LANES), F32)
    anywhere = pl.BlockSpec(memory_space=pl.ANY)
    dma = pltpu.SemaphoreType.DMA
    results = pl.pallas_call(
        functools.partial(kernel, size_x, size_y, size_s, ny * size_y),
        name="adjoint_steps",
        out_shape=(jax.ShapeDtypeStruct(adjoint_now.shape, F32), block, block, block),
        in_specs=[anywhere] * 9 + [pl.BlockSpec(memory_space=pltpu.SMEM), anywhere],
        out_specs=(anywhere,) * 4,
        scratch_shapes=[
            pltpu.VMEM((steps, nzb, 2, nx + 2, ny + 2 * TOP, LANES), F32),
            pltpu.VMEM((2, nx, ny, depth), F32),
            pltpu.VMEM((steps, 2, nx, ny, depth), BF16),
            pltpu.VMEM((2, nx, nzb, ny, LANES), F32),
            pltpu.VMEM((3, nx, ny, depth), F32),
            pltpu.VMEM((2, nx, ny, depth), jnp.int32),
            pltpu.VMEM((3, nx, ny, LANES), F32),
            pltpu.VMEM((1, channels), jnp.int32),
            pltpu.VMEM((steps, channels), F32),
            pltpu.VMEM((LANES, channels), F32),
            pltpu.VMEM((12, nx, nzb, ny, LANES), F32),
            pltpu.VMEM((steps, nx * ny, LANES), F32),
            pltpu.VMEM((2, nx, nzb, ny, LANES), F32),
            pltpu.VMEM((nzb, 2, nx, 3, ny // 2, LANES), F32),
            pltpu.VMEM((steps, 2, nx, 2 * nzb, LANES), F32),
            pltpu.VMEM((steps, 2, nx, 2 * nzb, LANES), F32),
            pltpu.VMEM((steps, 2, 2, 2 * nzb, LANES), F32),
            pltpu.VMEM((2, nx, 3, ny // 2, LANES), F32),
            pltpu.VMEM((2, 2, nx, 3, ny // 2, LANES), F32),
            pltpu.VMEM((2, nx, ny, depth), F32),
            pltpu.VMEM((3, nx, ny, LANES), F32),
            dma((nzb + 12,)),
            dma((4,)),
            dma((steps, 2)),
            dma((steps, 2)),
            dma((steps, 2, 2)),
            dma((steps, 2, 2)),
            dma((steps, 2, 2)),
            dma((steps, 2, 2)),
            dma((2, nx)),
            dma((2, nx)),
            dma((2, 2, nx)),
            dma((2, 2, nx)),
        ],
        compiler_params=pltpu.CompilerParams(
            collective_id=0, has_side_effects=True, vmem_limit_bytes=60 * 1024 * 1024
        ),
    )(
        adjoint_now,
        adjoint_before,
        forward_field,
        velocity,
        thomsen_eps,
        thomsen_delta,
        tilt_level,
        azimuth_level,
        channel_cell,
        channel_count,
        jnp.transpose(residual_trace, (1, 0, 2)),
    )
    return hand_out(results)


def solution(mesh):
    placed = (
        P("src", None, "gx", "gy", None),
        P("src", None, "gx", "gy", None),
        P(None, "src", None, "gx", "gy", None),
        P("gx", "gy", None),
        P("gx", "gy", None),
        P("gx", "gy", None),
        P("gx", "gy", None),
        P("gx", "gy", None),
        P("src", None),
        P("src"),
        P("src", None, None),
    )
    return jax.shard_map(
        on_device,
        mesh=mesh,
        in_specs=placed,
        out_specs=(
            P("src", None, "gx", "gy", None),
            P("gx", "gy", "src"),
            P("gx", "gy", "src"),
            P("gx", "gy", "src"),
        ),
        check_vma=False,
    )
```
